32 devices in a mesh: seq: 2 (over x), head: 4 (over z), pool: 4 (over y, core).
Axes of the slice: x: 2, y: 2, z: 4, core: 2. Of those that a mesh axis runs over, the one named last changes fastest.
Arguments:
- tokens: bfloat16 [32, 4096], P(('seq', 'head'), 'pool'), may hold values from -6 to 6
- routes: int32 [32, 8], P(('seq', 'head')), may hold values from 0 to 15, all different within a row; in each aligned block of 4 rows (0 to 3, 4 to 7, ...) at most 2 rows name the same one
- gate_fixed: int32 [32, 8], P(('seq', 'head')), may hold values from 1 to 65535
- gate_weight: bfloat16 [16, 4096, 3072], P('seq', 'pool', 'head'), may hold values from -0.09375 to 0.09375
- up_weight: bfloat16 [16, 4096, 3072], P('seq', 'pool', 'head'), may hold values from -0.09375 to 0.09375
- down_weight: bfloat16 [16, 3072, 4096], P('seq', 'head', 'pool'), may hold values from -0.109375 to 0.109375
- gate_scale: bfloat16 [16, 32, 24], P('seq', 'pool', 'head'), may hold values from 0.5 to 2
- up_scale: bfloat16 [16, 32, 24], P('seq', 'pool', 'head'), may hold values from 0.5 to 2
- down_scale: bfloat16 [16, 24, 32], P('seq', 'head', 'pool'), may hold values from 0.5 to 2
Outputs:
- combined: bfloat16 [32, 4096], P(('seq', 'head'), 'pool')
The draws below stay inside these ranges and needn't reach their ends.
Inputs may be any that keep to these rules, and one draw needn't show every extreme that they name: `routes`: each row names 8 different experts. Within the rows of one device (aligned blocks of 4 rows) no expert is named by more than 2 rows, and in some blocks one expert is named by exactly 2 rows.
All inputs are finite; a program needn't handle non-finite values.
Results may differ from the reference program's by a relative error of at most 0.02.
Values may be sent and summed in bfloat16 or wider, within the bound.
No kernel may reach another device: no remote copies, remote signals or barrier semaphores. Data moves between devices by JAX's collectives and lax.ppermute only.
A program may use at most 128 MiB of HBM per device.

```python
import math
import jax
import jax.numpy as jnp
import numpy as np
from jax import lax

D = 4096
FF = 3072
TOP = 8
QB = 128
ROWS_DEV = 4
CAP = 2
EXPERTS = 16
BLOCKS = 8
ROWS = 32
N_HEAD = 4
N_POOL = 4


def place_ends(entries, rng, low, top_value):
    longest = entries.shape.index(max(entries.shape))
    spots = []
    for shift in (0, 1):
        where = [jax.random.randint(jax.random.fold_in(rng, axis), (), 0, length) for axis, length in enumerate(entries.shape)]
        where[longest] = (where[longest] + shift) % entries.shape[longest]
        spots.append(tuple(where))
    return entries.at[spots[0]].set(low).at[spots[1]].set(top_value)


def block_levels(stream_key, extent, cuts, least, top_value):
    def one(dim, blocks):
        steps = jax.random.uniform(jax.random.fold_in(jax.random.fold_in(stream_key, 6), dim), (blocks,), jnp.float32, least / len(cuts), top_value / len(cuts))
        return jnp.repeat(jnp.exp(steps), extent[dim] // blocks).reshape((-1,) + (1,) * (len(extent) - dim - 1))

    level = one(*cuts[0])
    for cut in cuts[1:]:
        level = level * one(*cut)
    return level


def assign_block(key, own, number, rows, number_of, top, most, lean):
    ranking = jax.random.permutation(key, number_of)
    packed, usual = load_shares(number_of, rows * top, most, lean, True), load_shares(number_of, rows * top, most, lean, False)
    places = jnp.arange(number_of)

    def named(tallies, turn):
        used = int((tallies > 0).sum())
        fixed = max(1, used // 4)
        passed = fixed + (places - fixed + turn * (used - fixed)) % max(1, number_of - fixed)
        return jnp.zeros((number_of,), jnp.int32).at[ranking[jnp.where(places < fixed, places, passed)]].set(jnp.asarray(tallies, jnp.int32))

    tallies = jnp.where(number % 4 == 0, named(packed, number // 4), named(usual, number - number // 4 - 1))
    mixed = jax.random.permutation(jax.random.fold_in(own, 3), number_of)
    source_of, sink = mixed[0:number_of // 2 * 2:2], mixed[1:number_of // 2 * 2:2]
    margin = jnp.minimum(tallies[source_of] - 1, most - tallies[sink]) // 2
    margin = jnp.where((source_of == ranking[0]) | (sink == ranking[0]) | (tallies[sink] == 0), 0, jnp.maximum(margin, 0))
    passed = jax.random.randint(jax.random.fold_in(own, 4), (number_of // 2,), 0, 1 << 20) % (margin + 1)
    tallies = tallies.at[source_of].add(-passed).at[sink].add(passed)
    members = jnp.searchsorted(jnp.cumsum(tallies), jnp.arange(rows * top), side="right").astype(jnp.int32)
    grid = members.reshape(top, rows).T
    grid = grid[jax.random.permutation(jax.random.fold_in(own, 1), rows)]
    turn = jax.random.randint(jax.random.fold_in(own, 2), (rows, 1), 0, top)
    return jnp.take_along_axis(grid, (jnp.arange(top)[None, :] + turn) % top, axis=1)


def load_shares(amount, total, reach, skew, full):
    portions = [(1 << 20) // math.isqrt(rank ** skew) + 1 for rank in range(1, amount + 1)]
    largest = reach if full else min(reach, max(-(-total // amount), total * portions[0] // sum(portions)))
    least = 1 if total - largest >= amount - 1 else 0
    counts, rest = [largest] + [least] * (amount - 1), total - largest - least * (amount - 1)
    while rest > 0:
        candidates = [i for i in range(1, amount) if counts[i] < largest] or [i for i in range(1, amount) if counts[i] < reach]
        whole, remaining = sum([portions[i] for i in candidates]), rest
        for i in candidates:
            more = min(reach - counts[i], max(1, remaining * portions[i] // whole), rest)
            counts[i] = counts[i] + more
            rest = rest - more
    return np.array(counts)


def centred(stream_key, shape, deviation, limit, cuts=(), kind=jnp.bfloat16):
    entries = deviation * jax.random.normal(stream_key, shape, jnp.float32)
    if cuts:
        entries = entries * block_levels(stream_key, shape, cuts, -0.22, 0.18)
    return jnp.clip(entries, -limit, limit).astype(kind)


def setup_inputs(seed: int = 0) -> dict:
    key_of = jax.random.split(jax.random.key(seed), 10)
    tokens = centred(key_of[0], (ROWS, D), 1.0, 6.0, ((0, 8), (1, 4)))
    routes_keys = jax.random.split(jax.random.fold_in(key_of[1], 1), ROWS // ROWS_DEV)
    routes_turns = jax.random.permutation(jax.random.fold_in(key_of[1], 3), ROWS // ROWS_DEV)
    routes = jax.vmap(lambda own, number: assign_block(jax.random.fold_in(key_of[1], 2), own, number, ROWS_DEV, EXPERTS, TOP, CAP, 2))(routes_keys, routes_turns).reshape((ROWS, TOP))
    gate_fixed = place_ends(jax.random.randint(key_of[2], (ROWS, TOP), 1, 65536), jax.random.fold_in(key_of[2], 1), 1, 65535).astype(jnp.int32)
    gate_weight = centred(key_of[3], (EXPERTS, D, FF), D ** -0.5, 0.09375, ((0, 2), (1, 4), (2, 4)))
    up_weight = centred(key_of[4], (EXPERTS, D, FF), D ** -0.5, 0.09375, ((0, 2), (1, 4), (2, 4)))
    down_weight = centred(key_of[5], (EXPERTS, FF, D), FF ** -0.5, 0.109375, ((0, 2), (1, 4), (2, 4)))
    gate_scale = jnp.clip(jnp.exp(math.log(2.0) - 1.3862944 * jax.random.uniform(key_of[6], (EXPERTS, D // QB, FF // QB), jnp.float32) ** block_levels(key_of[6], (EXPERTS, D // QB, FF // QB), ((0, 2), (1, 4), (2, 4)), -0.2, 0.2)), 0.5, 2.0).astype(jnp.bfloat16)
    up_scale = jnp.clip(jnp.exp(math.log(2.0) - 1.3862944 * jax.random.uniform(key_of[7], (EXPERTS, D // QB, FF // QB), jnp.float32) ** block_levels(key_of[7], (EXPERTS, D // QB, FF // QB), ((0, 2), (1, 4), (2, 4)), -0.2, 0.2)), 0.5, 2.0).astype(jnp.bfloat16)
    down_scale = jnp.clip(jnp.exp(math.log(2.0) - 1.3862944 * jax.random.uniform(key_of[8], (EXPERTS, FF // QB, D // QB), jnp.float32) ** block_levels(key_of[8], (EXPERTS, FF // QB, D // QB), ((0, 2), (1, 4), (2, 4)), -0.2, 0.2)), 0.5, 2.0).astype(jnp.bfloat16)
    return dict(tokens=tokens, routes=routes, gate_fixed=gate_fixed, gate_weight=gate_weight, up_weight=up_weight, down_weight=down_weight, gate_scale=gate_scale, up_scale=up_scale, down_scale=down_scale)


largest_choice = lax.Precision.HIGHEST


def expand_scale(route_weight, scale):
    grown = jnp.repeat(jnp.repeat(scale.astype(jnp.float32), QB, axis=0), QB, axis=1)
    return (route_weight.astype(jnp.float32) * grown).astype(jnp.bfloat16)


def slot_positions(block_routes):
    flattened = block_routes.reshape(-1)
    expert_ids = jnp.arange(EXPERTS, dtype=jnp.int32)
    onehot = (flattened[:, None] == expert_ids[None, :]).astype(jnp.int32)
    before = jnp.cumsum(onehot, axis=0) - onehot
    slot_index = jnp.sum(before * onehot, axis=1)
    return (flattened * CAP + slot_index).reshape(block_routes.shape)


def expert_apply(operands):
    slot_rows, gate_weight, up_weight, down_weight, gate_scale, up_scale, down_scale = operands
    gate_dense = expand_scale(gate_weight, gate_scale)
    up_dense = expand_scale(up_weight, up_scale)
    down_dense = expand_scale(down_weight, down_scale)
    slot_count = slot_rows.shape[0]
    pooled = slot_rows.astype(jnp.float32).reshape(slot_count, N_POOL, D // N_POOL)

    def pool_sum(dense):
        grouped = dense.astype(jnp.float32).reshape(N_POOL, D // N_POOL, FF)
        partial_results = jnp.einsum("mpd,pdf->pmf", pooled, grouped, precision=largest_choice)
        rounded = lax.optimization_barrier(partial_results.astype(jnp.bfloat16))
        return jnp.sum(rounded.astype(jnp.float32), axis=0)

    gate_sum = pool_sum(gate_dense)
    up_sum = pool_sum(up_dense)
    hidden = (jax.nn.silu(gate_sum) * up_sum).astype(jnp.bfloat16)
    hidden_parts = hidden.astype(jnp.float32).reshape(slot_count, N_HEAD, FF // N_HEAD)
    down_by_expert = down_dense.astype(jnp.float32).reshape(N_HEAD, FF // N_HEAD, D)
    partial_results = jnp.einsum("vct,ctq->cvq", hidden_parts, down_by_expert, precision=largest_choice)
    rounded = lax.optimization_barrier(partial_results.astype(jnp.bfloat16))
    return jnp.sum(rounded.astype(jnp.float32), axis=0).astype(jnp.bfloat16)


def reference(tokens, routes, gate_fixed, gate_weight, up_weight, down_weight, gate_scale, up_scale, down_scale):
    blocked = routes.reshape(BLOCKS, ROWS_DEV, TOP)
    positions = jax.vmap(slot_positions)(blocked)
    targets = jnp.arange(EXPERTS * CAP, dtype=jnp.int32)
    matches = jnp.any(positions[:, :, :, None] == targets[None, None, None, :], axis=2).astype(jnp.int32)
    row_local = jnp.arange(ROWS_DEV, dtype=jnp.int32)
    found = jnp.sum(matches, axis=1)
    local_row = jnp.sum(matches * row_local[None, :, None], axis=1)
    block_start = (jnp.arange(BLOCKS, dtype=jnp.int32) * ROWS_DEV)[:, None]
    source = jnp.where(found > 0, block_start + local_row, ROWS).astype(jnp.int32)
    padded = jnp.concatenate([tokens, jnp.zeros((1, D), tokens.dtype)], axis=0)
    gathered = padded[source]
    per_expert = gathered.reshape(BLOCKS, EXPERTS, CAP, D).transpose(1, 0, 2, 3).reshape(EXPERTS, BLOCKS * CAP, D)
    outputs = lax.map(expert_apply, (per_expert, gate_weight, up_weight, down_weight, gate_scale, up_scale, down_scale))
    outputs = outputs.reshape(EXPERTS, BLOCKS, CAP, D)
    slot_index = (positions - blocked * CAP).astype(jnp.int32)
    block_ids = jnp.arange(BLOCKS, dtype=jnp.int32)[:, None, None]
    picked = outputs[blocked, block_ids, slot_index]
    fixed = gate_fixed.astype(jnp.float32).reshape(BLOCKS, ROWS_DEV, TOP)
    weights = fixed / jnp.sum(fixed, axis=2, keepdims=True)
    combined = jnp.sum(weights[..., None] * picked.astype(jnp.float32), axis=2)
    return combined.reshape(ROWS, D).astype(jnp.bfloat16)
```

```python
import functools

import jax
import jax.numpy as jnp
from jax import lax
from jax.experimental import pallas as pl
from jax.experimental.pallas import tpu as pltpu
from jax.sharding import PartitionSpec as P

QB = 128
CAP = 2
LANES = 128
BF = jnp.bfloat16
F32 = jnp.float32
I32 = jnp.int32

VM = pl.BlockSpec(memory_space=pltpu.VMEM)
SM = pl.BlockSpec(memory_space=pltpu.SMEM)
HB = pl.BlockSpec(memory_space=pltpu.HBM)


def sds(shape, dtype):
    return jax.ShapeDtypeStruct(shape, dtype)


def run(kernel, out_shape, in_specs, args, name, limit=2 << 20, flops=0, bytes_=0, **more):
    outs = out_shape if isinstance(out_shape, (list, tuple)) else [out_shape]
    specs = [VM] * len(outs)
    return pl.pallas_call(
        kernel,
        out_shape=out_shape,
        in_specs=in_specs,
        out_specs=specs if isinstance(out_shape, (list, tuple)) else VM,
        compiler_params=pltpu.CompilerParams(vmem_limit_bytes=limit),
        cost_estimate=pl.CostEstimate(flops=flops, bytes_accessed=bytes_, transcendentals=0),
        name=name,
        **more,
    )(*args)


def iota(shape, dim):
    return lax.broadcasted_iota(I32, shape, dim)


def placed(values, start):
    n = values.shape[1]
    spot = (iota((n, LANES), 1) == iota((n, LANES), 0) + start).astype(BF)
    return jnp.dot(values.astype(F32).astype(BF), spot, preferred_element_type=F32)


def pack(tokens, routes, gates, scales):
    rows, width = tokens.shape
    top = routes.shape[1]

    def kernel(t_in, r_in, g_in, *rest):
        s_in, (x_out, *s_out) = rest[:3], rest[3:7]
        t_v, r_v, g_v, *s_v = rest[7:13]
        sems = rest[13]
        copies = [
            pltpu.make_async_copy(src, dst, sems.at[i])
            for i, (src, dst) in enumerate(
                zip((r_in, g_in, t_in, *s_in), (r_v, g_v, t_v, *s_v))
            )
        ]
        for copy in copies:
            copy.start()
        for copy in copies:
            copy.wait()
        x_out[:, :width] = t_v[...]
        gate = g_v[...]
        meta = (
            placed(r_v[...], 0)
            + placed(lax.shift_right_logical(gate, 8), top)
            + placed(gate & 255, 2 * top)
        )
        x_out[:, width:] = meta.astype(BF)
        for src, dst in zip(s_v, s_out):
            dst[...] = src[...].astype(F32)

    arrays = (tokens, routes, gates, *scales)
    return run(
        kernel,
        [sds((rows, width + LANES), BF)] + [sds(s.shape, F32) for s in scales],
        [HB] * len(arrays),
        arrays,
        "pack",
        scratch_shapes=[pltpu.VMEM(a.shape, a.dtype) for a in arrays]
        + [pltpu.SemaphoreType.DMA((len(arrays),))],
    )


def cat(a, b):
    rows = a.shape[0]

    def kernel(a_ref, b_ref, o_ref):
        o_ref[:rows] = a_ref[...]
        o_ref[rows:] = b_ref[...]

    return run(kernel, sds((2 * rows,) + a.shape[1:], a.dtype), [VM] * 2, (a, b), "cat")


def dispatch(x, width, top, rows_dev, experts, slots):
    rows = x.shape[0]
    per = slots // experts
    meta = x[:, width:].astype(F32)
    base = (lax.axis_index("seq") * experts).astype(F32)
    lane = iota((rows, LANES), 1)
    named = jnp.where(lane < experts, lane, -LANES).astype(F32) + base
    hits = jnp.zeros((rows, LANES), F32)
    gates = jnp.zeros((rows, LANES), F32)
    total = jnp.zeros((rows, 1), F32)
    for k in range(top):
        gate = meta[:, top + k : top + k + 1] * 256.0 + meta[:, 2 * top + k : 2 * top + k + 1]
        equal = meta[:, k : k + 1] == named
        hits = hits + jnp.where(equal, 1.0, 0.0)
        gates = gates + jnp.where(equal, gate, 0.0)
        total = total + gate
    weights = gates / total
    r0, r1 = iota((rows, rows), 0), iota((rows, rows), 1)
    earlier = ((r0 // rows_dev == r1 // rows_dev) & (r1 < r0)).astype(BF)
    rank = jnp.dot(earlier, hits.astype(BF), preferred_element_type=F32)
    grow = (iota((LANES, slots), 1) // per == iota((LANES, slots), 0)).astype(BF)
    wide_hits = jnp.dot(hits.astype(BF), grow, preferred_element_type=F32)
    wide_rank = jnp.dot(rank.astype(BF), grow, preferred_element_type=F32)
    spot = (iota((rows, slots), 1) % per - (iota((rows, slots), 0) // rows_dev) * CAP).astype(F32)
    sel = jnp.where((wide_hits > 0.5) & (wide_rank == spot), 1.0, 0.0).astype(BF)
    slot_rows = lax.dot_general(
        sel, x[:, :width], (((0,), (0,)), ((), ())), preferred_element_type=F32
    ).astype(BF)
    return sel, weights, slot_rows


def scaled(w, scale, e, d, f, d_blk, f_blk):
    block = w[e, pl.ds(d, QB), pl.ds(f, QB)]
    return block * scale[e, d_blk, f_blk].astype(BF)


def half_products(xs_ref, gw, uw, gs, us, o_ref, half):
    experts, width, hidden = gw.shape
    n = hidden // 2 // QB
    per = xs_ref.shape[0] // experts
    columns = [(gw, gs, j) for j in range(n)] + [(uw, us, j) for j in range(n)]
    starts = [pl.multiple_of((half * n + j) * QB, QB) for j in range(n)]
    group, deep = (2 if n % 1 == 0 else 1), 2 * QB
    for e in range(experts):
        xs = xs_ref[e * per : (e + 1) * per, :]
        for at in range(0, len(columns), group):
            acc = jnp.zeros((per, group * QB), F32)
            for d in range(0, width, deep):
                rhs = jnp.concatenate(
                    [
                        jnp.concatenate(
                            [
                                scaled(w, s, e, d + q, starts[j], (d + q) // QB, half * n + j)
                                for w, s, j in columns[at : at + group]
                            ],
                            axis=1,
                        )
                        for q in range(0, deep, QB)
                    ],
                    axis=0,
                )
                acc = acc + jnp.dot(xs[:, d : d + deep], rhs, preferred_element_type=F32)
            o_ref[e * per : (e + 1) * per, at * QB : (at + group) * QB] = acc.astype(o_ref.dtype)


def other_half(x, gw, uw, gs, us, top, rows_dev, blocks):
    experts, width, hidden = gw.shape
    rows = x.shape[0]
    slots = experts * blocks * CAP

    def kernel(x_ref, gw_ref, uw_ref, gs_ref, us_ref, o_ref, xs_ref, sel_ref, wt_ref):
        sel, weights, slot_rows = dispatch(x_ref[...], width, top, rows_dev, experts, slots)
        sel_ref[...] = sel
        wt_ref[...] = weights
        xs_ref[...] = slot_rows
        half = 1 - lax.rem(lax.axis_index("pool"), 2)
        half_products(xs_ref, gw_ref, uw_ref, gs_ref, us_ref, o_ref, half)

    return run(
        kernel,
        [sds((slots, hidden), BF), sds((slots, width), BF), sds((rows, slots), BF), sds((rows, LANES), F32)],
        [VM] * 3 + [SM] * 2,
        (x, gw, uw, gs, us),
        "other_half",
        limit=8 << 20,
        flops=2 * slots * width * hidden,
        bytes_=2 * experts * width * hidden,
    )


def own_half(xs, gw, uw, gs, us):
    experts, width, hidden = gw.shape
    slots = xs.shape[0]

    def kernel(xs_ref, gw_ref, uw_ref, gs_ref, us_ref, o_ref):
        half = lax.rem(lax.axis_index("pool"), 2)
        half_products(xs_ref, gw_ref, uw_ref, gs_ref, us_ref, o_ref, half)

    return run(
        kernel,
        sds((slots, hidden), F32),
        [VM] * 3 + [SM] * 2,
        (xs, gw, uw, gs, us),
        "own_half",
        limit=8 << 20,
        flops=2 * slots * width * hidden,
        bytes_=2 * experts * width * hidden,
    )


def add_round(own, got):
    def kernel(a_ref, b_ref, o_ref, r_ref):
        total = a_ref[...] + b_ref[...].astype(F32)
        o_ref[...] = total
        r_ref[...] = total.astype(BF)

    return run(kernel, [sds(own.shape, F32), sds(own.shape, BF)], [VM] * 2, (own, got), "add_round")


def activate(own, got):
    slots, hidden = own.shape
    n = hidden // 2

    def kernel(a_ref, b_ref, o_ref):
        gate = a_ref[:, :n] + b_ref[:, :n].astype(F32)
        up = a_ref[:, n:] + b_ref[:, n:].astype(F32)
        o_ref[...] = (jax.nn.silu(gate) * up).astype(BF)

    return run(kernel, sds((slots, n), BF), [VM] * 2, (own, got), "activate")


def down_products(h_ref, sel_ref, wt_ref, dw, ds, half):
    experts, hidden, width = dw.shape
    rows, slots = sel_ref.shape
    per = slots // experts
    n = hidden // 2 // QB
    sel = sel_ref[...].astype(F32)
    owner = iota((rows, slots), 1) // per
    stack = jnp.concatenate([jnp.where(owner == e, sel, 0.0) for e in range(experts)], axis=0)
    spread = jnp.dot(stack.astype(BF), h_ref[...], preferred_element_type=F32)
    weights = wt_ref[...]
    pieces = []
    for e in range(experts):
        part = spread[e * rows : (e + 1) * rows] * weights[:, e : e + 1]
        part = part.astype(BF)
        pieces += [(e, j, part[:, j * QB : (j + 1) * QB]) for j in range(n)]
    starts = [pl.multiple_of((half * n + j) * QB, QB) for j in range(n)]
    deep = 2 if len(pieces) % 2 == 0 else 1
    group = 2
    outs = []
    for c in range(0, width // QB, group):
        acc = jnp.zeros((rows, group * QB), F32)
        for at in range(0, len(pieces), deep):
            use = pieces[at : at + deep]
            lhs = jnp.concatenate([p for _, _, p in use], axis=1)
            rhs = jnp.concatenate(
                [
                    jnp.concatenate(
                        [
                            scaled(dw, ds, e, starts[j], (c + q) * QB, half * n + j, c + q)
                            for q in range(group)
                        ],
                        axis=1,
                    )
                    for e, j, _ in use
                ],
                axis=0,
            )
            acc = acc + jnp.dot(lhs, rhs, preferred_element_type=F32)
        outs.append(acc)
    return outs


def down_own(hid, sel, wt, dw, ds):
    experts, hidden, width = dw.shape
    rows = sel.shape[0]

    def kernel(h_ref, sel_ref, wt_ref, dw_ref, ds_ref, o_ref):
        half = lax.rem(lax.axis_index("pool"), 2)
        for i, acc in enumerate(down_products(h_ref, sel_ref, wt_ref, dw_ref, ds_ref, half)):
            o_ref[:, i * 2 * QB : (i + 1) * 2 * QB] = acc

    return run(
        kernel,
        sds((rows, width), F32),
        [VM] * 4 + [SM],
        (hid, sel, wt, dw, ds),
        "down_own",
        limit=8 << 20,
        flops=experts * rows * width * hidden,
        bytes_=experts * width * hidden,
    )


def down_other(hid, sel, wt, dw, ds, own):
    experts, hidden, width = dw.shape
    rows = sel.shape[0]
    keep = rows // 2

    def kernel(h_ref, sel_ref, wt_ref, dw_ref, ds_ref, a_ref, o_ref, s_ref):
        half = 1 - lax.rem(lax.axis_index("pool"), 2)
        for i, acc in enumerate(down_products(h_ref, sel_ref, wt_ref, dw_ref, ds_ref, half)):
            at = slice(i * 2 * QB, (i + 1) * 2 * QB)
            total = acc + a_ref[:, at]
            o_ref[:, at] = total[:keep]
            s_ref[:, at] = total[keep:].astype(BF)

    return run(
        kernel,
        [sds((keep, width), F32), sds((rows - keep, width), BF)],
        [VM] * 4 + [SM, VM],
        (hid, sel, wt, dw, ds, own),
        "down_other",
        limit=8 << 20,
        flops=experts * rows * width * hidden,
        bytes_=experts * width * hidden,
    )


def fold(own, got):
    rows, width = own.shape
    keep = rows // 2

    def kernel(a_ref, b_ref, o_ref, s_ref):
        o_ref[...] = a_ref[:keep] + b_ref[:keep].astype(F32)
        s_ref[...] = (a_ref[keep:] + b_ref[keep:].astype(F32)).astype(BF)

    return run(
        kernel, [sds((keep, width), F32), sds((keep, width), BF)], [VM] * 2, (own, got), "fold"
    )


def finish(own, got):
    def kernel(a_ref, b_ref, o_ref):
        o_ref[...] = (a_ref[...] + b_ref[...].astype(F32)).astype(BF)

    return run(kernel, sds(own.shape, BF), [VM] * 2, (own, got), "finish")


def swap(x, axis, bit):
    return lax.ppermute(x, axis, [(j, j ^ bit) for j in range(lax.axis_size(axis))])


def bits(count):
    return [1 << i for i in range(count.bit_length() - 1)]


def per_device(tokens, routes, gate_fixed, gw, uw, dw, gs, us, ds):
    n_seq, n_head, n_pool = (lax.axis_size(a) for a in ("seq", "head", "pool"))
    rows_dev, width = tokens.shape
    top = routes.shape[1]
    hops = [("head", b) for b in reversed(bits(n_head))] + [("seq", b) for b in bits(n_seq)]

    gw, uw, dw = (pltpu.with_memory_space_constraint(w, pltpu.VMEM) for w in (gw, uw, dw))
    x, gs, us, ds = pack(tokens, routes, gate_fixed, (gs, us, ds))
    for axis, bit in hops:
        x = cat(x, swap(x, axis, bit))

    send, xs, sel, wt = other_half(x, gw, uw, gs, us, top, rows_dev, n_seq * n_head)
    got = swap(send, "pool", 1)
    own = own_half(xs, gw, uw, gs, us)
    for bit in bits(n_pool)[1:]:
        own, send = add_round(own, got)
        got = swap(send, "pool", bit)
    hid = activate(own, got)
    other = swap(hid, "pool", 1)
    acc = down_own(hid, sel, wt, dw, ds)
    acc, send = down_other(other, sel, wt, dw, ds, acc)
    for axis, bit in reversed(hops[1:]):
        acc, send = fold(acc, swap(send, axis, bit))
    axis, bit = hops[0]
    return finish(acc, swap(send, axis, bit))


def solution(mesh):
    return jax.shard_map(
        per_device,
        mesh=mesh,
        in_specs=(
            P(("seq", "head"), "pool"),
            P(("seq", "head"), None),
            P(("seq", "head"), None),
            P("seq", "pool", "head"),
            P("seq", "pool", "head"),
            P("seq", "head", "pool"),
            P("seq", "pool", "head"),
            P("seq", "pool", "head"),
            P("seq", "head", "pool"),
        ),
        out_specs=P(("seq", "head"), "pool"),
        check_vma=False,
    )
```

```python
import functools

import jax
import jax.numpy as jnp
from jax import lax
from jax.experimental import pallas as pl
from jax.experimental.pallas import tpu as pltpu
from jax.sharding import PartitionSpec as P

QB = 128
CAP = 2
LANES = 128
BF = jnp.bfloat16
F32 = jnp.float32
I32 = jnp.int32

VM = pl.BlockSpec(memory_space=pltpu.VMEM)
SM = pl.BlockSpec(memory_space=pltpu.SMEM)
HB = pl.BlockSpec(memory_space=pltpu.HBM)


def sds(shape, dtype):
    return jax.ShapeDtypeStruct(shape, dtype)


def run(kernel, out_shape, in_specs, args, name, limit=2 << 20, flops=0, bytes_=0, **more):
    outs = out_shape if isinstance(out_shape, (list, tuple)) else [out_shape]
    specs = [VM] * len(outs)
    return pl.pallas_call(
        kernel,
        out_shape=out_shape,
        in_specs=in_specs,
        out_specs=specs if isinstance(out_shape, (list, tuple)) else VM,
        compiler_params=pltpu.CompilerParams(vmem_limit_bytes=limit),
        cost_estimate=pl.CostEstimate(flops=flops, bytes_accessed=bytes_, transcendentals=0),
        name=name,
        **more,
    )(*args)


def in_hbm(a):
    return pltpu.with_memory_space_constraint(a, pltpu.HBM)


def in_vmem(a):
    return pltpu.with_memory_space_constraint(a, pltpu.VMEM)


def iota(shape, dim):
    return lax.broadcasted_iota(I32, shape, dim)


def placed(values, start):
    n = values.shape[1]
    spot = (iota((n, LANES), 1) == iota((n, LANES), 0) + start).astype(BF)
    return jnp.dot(values.astype(F32).astype(BF), spot, preferred_element_type=F32)


def pack(tokens, routes, gates, scales):
    rows, width = tokens.shape
    top = routes.shape[1]

    def kernel(t_in, r_in, g_in, *rest):
        s_in, (x_out, *s_out) = rest[:3], rest[3:7]
        t_v, r_v, g_v, *s_v = rest[7:13]
        sems = rest[13]
        copies = [
            pltpu.make_async_copy(src, dst, sems.at[i])
            for i, (src, dst) in enumerate(
                zip((r_in, g_in, t_in, *s_in), (r_v, g_v, t_v, *s_v))
            )
        ]
        for copy in copies:
            copy.start()
        for copy in copies:
            copy.wait()
        x_out[:, :width] = t_v[...]
        gate = g_v[...]
        meta = (
            placed(r_v[...], 0)
            + placed(lax.shift_right_logical(gate, 8), top)
            + placed(gate & 255, 2 * top)
        )
        x_out[:, width:] = meta.astype(BF)
        for src, dst in zip(s_v, s_out):
            dst[...] = src[...].astype(F32)

    arrays = (tokens, routes, gates, *scales)
    arrays = [in_hbm(a) for a in arrays]
    return run(
        kernel,
        [sds((rows, width + LANES), BF)] + [sds(s.shape, F32) for s in scales],
        [HB] * len(arrays),
        arrays,
        "pack",
        scratch_shapes=[pltpu.VMEM(a.shape, a.dtype) for a in arrays]
        + [pltpu.SemaphoreType.DMA((len(arrays),))],
    )


def cat(a, b, after):
    rows = a.shape[0]

    def kernel(a_ref, b_ref, *rest):
        o_ref = rest[-1]
        o_ref[:rows] = a_ref[...]
        o_ref[rows:] = b_ref[...]

    return run(
        kernel,
        sds((2 * rows,) + a.shape[1:], a.dtype),
        [VM] * (2 + len(after)),
        (a, b, *after),
        "cat",
    )


def load(sources, after):
    shape = sources[0][0].shape[1:]
    count = len(sources)
    arrays = []
    for w, _ in sources:
        if not any(w is a for a in arrays):
            arrays.append(w)
    where = [([w is a for a in arrays].index(True), e) for w, e in sources]

    def kernel(*refs):
        w_refs, (o_ref, t_ref, sems) = refs[: len(arrays)], refs[len(arrays) + 1 :]
        copies = [
            pltpu.make_async_copy(w_refs[k].at[e], o_ref.at[i], sems.at[i])
            for i, (k, e) in enumerate(where)
        ]
        for copy in copies:
            copy.start()
        t_ref[...] = jnp.zeros_like(t_ref)
        for copy in copies:
            copy.wait()

    moved = 2 * count * shape[0] * shape[1]
    return pl.pallas_call(
        kernel,
        out_shape=[pltpu.VMEM((count,) + shape, BF), sds((8, LANES), F32)],
        in_specs=[HB] * len(arrays) + [VM],
        out_specs=[VM, VM],
        scratch_shapes=[pltpu.SemaphoreType.DMA((count,))],
        compiler_params=pltpu.CompilerParams(vmem_limit_bytes=1 << 20),
        cost_estimate=pl.CostEstimate(flops=0, bytes_accessed=2 * moved, transcendentals=0),
        name="load",
    )(*[in_hbm(a) for a in arrays], after)


def dispatch(x, width, top, rows_dev, experts, slots):
    rows = x.shape[0]
    per = slots // experts
    meta = x[:, width:].astype(F32)
    base = (lax.axis_index("seq") * experts).astype(F32)
    lane = iota((rows, LANES), 1)
    named = jnp.where(lane < experts, lane, -LANES).astype(F32) + base
    hits = jnp.zeros((rows, LANES), F32)
    gates = jnp.zeros((rows, LANES), F32)
    total = jnp.zeros((rows, 1), F32)
    for k in range(top):
        gate = meta[:, top + k : top + k + 1] * 256.0 + meta[:, 2 * top + k : 2 * top + k + 1]
        equal = meta[:, k : k + 1] == named
        hits = hits + jnp.where(equal, 1.0, 0.0)
        gates = gates + jnp.where(equal, gate, 0.0)
        total = total + gate
    weights = gates / total
    r0, r1 = iota((rows, rows), 0), iota((rows, rows), 1)
    earlier = ((r0 // rows_dev == r1 // rows_dev) & (r1 < r0)).astype(BF)
    rank = jnp.dot(earlier, hits.astype(BF), preferred_element_type=F32)
    grow = (iota((LANES, slots), 1) // per == iota((LANES, slots), 0)).astype(BF)
    wide_hits = jnp.dot(hits.astype(BF), grow, preferred_element_type=F32)
    wide_rank = jnp.dot(rank.astype(BF), grow, preferred_element_type=F32)
    spot = (iota((rows, slots), 1) % per - (iota((rows, slots), 0) // rows_dev) * CAP).astype(F32)
    sel = jnp.where((wide_hits > 0.5) & (wide_rank == spot), 1.0, 0.0).astype(BF)
    slot_rows = lax.dot_general(
        sel, x[:, :width], (((0,), (0,)), ((), ())), preferred_element_type=F32
    ).astype(BF)
    return sel, weights, slot_rows


class Blocks:
    def __init__(self, held_refs, held_at, streams, rows_cut, half, n):
        self.held_refs, self.held_at, self.streams = held_refs, held_at, streams
        self.rows_cut, self.half, self.n = rows_cut, half, n
        self.starts = [pl.multiple_of((half * n + j) * QB, QB) for j in range(n)]

    def start(self):
        for copy in self.streams.values():
            copy[0].start()

    def arrive(self, key):
        if key in self.streams:
            self.streams[key][0].wait()

    def get(self, key, j, k):
        far = pl.ds(k * QB, QB)
        if key in self.held_at:
            ref, at = self.held_at[key]
            near = pl.ds(self.starts[j], QB)
            ref = self.held_refs[ref]
        else:
            ref, at = self.streams[key][1:]
            near = pl.ds(j * QB, QB)
        return ref[at, near, far] if self.rows_cut else ref[at, far, near]


def blocks_of(held_refs, held_at, sources, buf, sems, rows_cut, half, n):
    streams = {}
    for i, (key, ref, e) in enumerate(sources):
        cut = pl.ds(pl.multiple_of(half * (n * QB), QB), n * QB)
        src = ref.at[e, cut, :] if rows_cut else ref.at[e, :, cut]
        streams[key] = (pltpu.make_async_copy(src, buf.at[i], sems.at[i]), buf, i)
    return Blocks(held_refs, held_at, streams, rows_cut, half, n)


def tile(parts):
    return jnp.concatenate([jnp.concatenate(row, axis=1) for row in parts], axis=0)


def half_products(xs_ref, blocks, scales, o_ref, experts):
    width = xs_ref.shape[1]
    n, half = blocks.n, blocks.half
    per = xs_ref.shape[0] // experts
    columns = [(0, j) for j in range(n)] + [(1, j) for j in range(n)]
    group, deep = 2, 2
    for e in range(experts):
        xs = xs_ref[e * per : (e + 1) * per, :]
        blocks.arrive((0, e))
        blocks.arrive((1, e))
        for at in range(0, len(columns), group):
            acc = jnp.zeros((per, group * QB), F32)
            for d in range(0, width // QB, deep):
                rhs = tile(
                    [
                        [
                            blocks.get((m, e), j, q) * scales[m][half * n + j, e, q].astype(BF)
                            for m, j in columns[at : at + group]
                        ]
                        for q in range(d, d + deep)
                    ]
                )
                acc = acc + jnp.dot(
                    xs[:, d * QB : (d + deep) * QB], rhs, preferred_element_type=F32
                )
            o_ref[e * per : (e + 1) * per, at * QB : (at + group) * QB] = acc.astype(o_ref.dtype)


def up_kernel(first, x, gw, uw, gs, us, held, held_at, top, rows_dev, block_count):
    experts, width, hidden = gw.shape
    n = hidden // 2 // QB
    slots = experts * block_count * CAP
    rows = block_count * rows_dev
    streamed = [(m, e) for e in range(experts) for m in (0, 1) if (m, e) not in held_at]

    def kernel(x_ref, gw_ref, uw_ref, gs_ref, us_ref, *rest):
        held_refs, rest = rest[: len(held)], rest[len(held) :]
        outs, (buf, sems) = rest[:-2], rest[-2:]
        half = lax.rem(lax.axis_index("pool"), 2)
        half = 1 - half if first else half
        sources = [((m, e), (gw_ref, uw_ref)[m], e) for m, e in streamed]
        blocks = blocks_of(held_refs, held_at, sources, buf, sems, False, half, n)
        blocks.start()
        if first:
            o_ref, xs_ref, sel_ref, wt_ref = outs
            sel, weights, slot_rows = dispatch(x_ref[...], width, top, rows_dev, experts, slots)
            sel_ref[...] = sel
            wt_ref[...] = weights
            xs_ref[...] = slot_rows
        else:
            (o_ref,) = outs
            xs_ref = x_ref
        half_products(xs_ref, blocks, (gs_ref, us_ref), o_ref, experts)

    products = sds((slots, hidden), BF if first else F32)
    more = [sds((slots, width), BF), sds((rows, slots), BF), sds((rows, LANES), F32)]
    return run(
        kernel,
        [products] + more if first else products,
        [VM, HB, HB, SM, SM] + [VM] * len(held),
        (x, in_hbm(gw), in_hbm(uw), gs, us, *[in_vmem(h) for h in held]),
        "other_half" if first else "own_half",
        limit=24 << 20,
        flops=2 * slots * width * hidden,
        bytes_=2 * experts * width * hidden,
        scratch_shapes=[
            pltpu.VMEM((max(1, len(streamed)), width, hidden // 2), BF),
            pltpu.SemaphoreType.DMA((max(1, len(streamed)),)),
        ],
    )


def add_round(own, got):
    def kernel(a_ref, b_ref, o_ref, r_ref):
        total = a_ref[...] + b_ref[...].astype(F32)
        o_ref[...] = total
        r_ref[...] = total.astype(BF)

    return run(kernel, [sds(own.shape, F32), sds(own.shape, BF)], [VM] * 2, (own, got), "add_round")


def activate(own, got, after):
    slots, hidden = own.shape
    n = hidden // 2

    def kernel(a_ref, b_ref, *rest):
        o_ref = rest[-1]
        gate = a_ref[:, :n] + b_ref[:, :n].astype(F32)
        up = a_ref[:, n:] + b_ref[:, n:].astype(F32)
        o_ref[...] = (jax.nn.silu(gate) * up).astype(BF)

    return run(
        kernel,
        sds((slots, n), BF),
        [VM] * (2 + len(after)),
        (own, got, *after),
        "activate",
    )


def spread_rows(h_ref, sel_ref, wt_ref, experts):
    rows, slots = sel_ref.shape
    per = slots // experts
    sel = sel_ref[...].astype(F32)
    owner = iota((rows, slots), 1) // per
    stack = jnp.concatenate([jnp.where(owner == e, sel, 0.0) for e in range(experts)], axis=0)
    spread = jnp.dot(stack.astype(BF), h_ref[...], preferred_element_type=F32)
    weights = wt_ref[...]
    return [
        (spread[e * rows : (e + 1) * rows] * weights[:, e : e + 1]).astype(BF)
        for e in range(experts)
    ]


def down_products(parts, blocks, scale, experts, width, put):
    n, half, group = blocks.n, blocks.half, 2
    pieces = [(e, j) for e in range(experts) for j in range(n)]
    kept = [p for p in pieces if p[0] in blocks.held_at]
    rest = [p for p in pieces if p[0] not in blocks.held_at]
    for use in (kept, rest):
        if not use:
            continue
        for e in sorted({e for e, _ in use}):
            blocks.arrive(e)
        deep = 2 if len(use) % 2 == 0 else 1
        for c in range(0, width // QB, group):
            acc = None
            for at in range(0, len(use), deep):
                some = use[at : at + deep]
                lhs = jnp.concatenate([parts[e][:, j * QB : (j + 1) * QB] for e, j in some], axis=1)
                rhs = tile(
                    [
                        [
                            blocks.get(e, j, q) * scale[half * n + j, e, q].astype(BF)
                            for q in range(c, c + group)
                        ]
                        for e, j in some
                    ]
                )
                more = jnp.dot(lhs, rhs, preferred_element_type=F32)
                acc = more if acc is None else acc + more
            put(slice(c * QB, (c + group) * QB), acc, use is kept or not kept)


def down_kernel(hid, sel, wt, dw, ds, held, held_at, own):
    experts, hidden, width = dw.shape
    n = hidden // 2 // QB
    rows = sel.shape[0]
    keep = rows // 2
    last = own is not None
    streamed = [e for e in range(experts) if e not in held_at]
    given = [own] if last else []

    def kernel(h_ref, sel_ref, wt_ref, dw_ref, ds_ref, *rest):
        held_refs, rest = rest[: len(held)], rest[len(held) :]
        given_refs, rest = rest[: len(given)], rest[len(given) :]
        outs, (total, buf, sems) = rest[:-3], rest[-3:]
        half = lax.rem(lax.axis_index("pool"), 2)
        half = 1 - half if last else half
        sources = [(e, dw_ref, e) for e in streamed]
        blocks = blocks_of(held_refs, held_at, sources, buf, sems, True, half, n)
        blocks.start()
        parts = spread_rows(h_ref, sel_ref, wt_ref, experts)
        o_ref = total if last else outs[0]

        def put(at, acc, fresh):
            if not fresh:
                acc = acc + o_ref[:, at]
            elif last:
                acc = acc + given_refs[0][:, at]
            o_ref[:, at] = acc

        down_products(parts, blocks, ds_ref, experts, width, put)
        if last:
            outs[0][...] = total[:keep]
            outs[1][...] = total[keep:].astype(BF)

    return run(
        kernel,
        [sds((keep, width), F32), sds((rows - keep, width), BF)] if last else sds((rows, width), F32),
        [VM, VM, VM, HB, SM] + [VM] * (len(held) + len(given)),
        (hid, sel, wt, in_hbm(dw), ds, *[in_vmem(h) for h in held], *given),
        "down_other" if last else "down_own",
        limit=24 << 20,
        flops=experts * rows * width * hidden,
        bytes_=experts * width * hidden,
        scratch_shapes=[
            pltpu.VMEM((rows if last else 8, width), F32),
            pltpu.VMEM((max(1, len(streamed)), hidden // 2, width), BF),
            pltpu.SemaphoreType.DMA((max(1, len(streamed)),)),
        ],
    )


def fold(own, got):
    rows, width = own.shape
    keep = rows // 2

    def kernel(a_ref, b_ref, o_ref, s_ref):
        o_ref[...] = a_ref[:keep] + b_ref[:keep].astype(F32)
        s_ref[...] = (a_ref[keep:] + b_ref[keep:].astype(F32)).astype(BF)

    return run(
        kernel, [sds((keep, width), F32), sds((keep, width), BF)], [VM] * 2, (own, got), "fold"
    )


def finish(own, got):
    def kernel(a_ref, b_ref, o_ref):
        o_ref[...] = (a_ref[...] + b_ref[...].astype(F32)).astype(BF)

    return run(kernel, sds(own.shape, BF), [VM] * 2, (own, got), "finish")


def swap(x, axis, bit):
    return lax.ppermute(x, axis, [(j, j ^ bit) for j in range(lax.axis_size(axis))])


def bits(count):
    return [1 << i for i in range(count.bit_length() - 1)]


def per_device(tokens, routes, gate_fixed, gw, uw, dw, gs, us, ds):
    n_seq, n_head, n_pool = (lax.axis_size(a) for a in ("seq", "head", "pool"))
    rows_dev, width = tokens.shape
    top = routes.shape[1]
    hops = [("head", b) for b in reversed(bits(n_head))] + [("seq", b) for b in bits(n_seq)]

    experts = gw.shape[0]
    scales = [gs.transpose(2, 0, 1), us.transpose(2, 0, 1), ds.transpose(1, 0, 2)]
    x, gs, us, ds = pack(tokens, routes, gate_fixed, scales)
    waiting = [(m, e) for e in range(experts // 2) for m in (0, 1)]
    held, held_at = [], {}
    for i, (axis, bit) in enumerate(hops):
        got = swap(x, axis, bit)
        take = -(-len(waiting) // (len(hops) - i))
        after = []
        if take:
            use, waiting = waiting[:take], waiting[take:]
            block, token = load([((gw, uw)[m], e) for m, e in use], x)
            held_at.update({key: (len(held), at) for at, key in enumerate(use)})
            held.append(block)
            after = [token]
        x = cat(x, got, after)

    common = (gw, uw, gs, us, held, held_at, top, rows_dev, n_seq * n_head)
    send, xs, sel, wt = up_kernel(True, x, *common)
    got = swap(send, "pool", 1)
    own = up_kernel(False, xs, *common)
    steps = bits(n_pool)[1:]
    waiting = list(range(experts * 3 // 4))
    held, held_at = [], {}
    tokens_of = []
    for i, bit in enumerate(steps):
        own, send = add_round(own, got)
        got = swap(send, "pool", bit)
        take = -(-len(waiting) // (len(steps) - i))
        if take:
            use, waiting = waiting[:take], waiting[take:]
            block, token = load([(dw, e) for e in use], send)
            held_at.update({e: (len(held), at) for at, e in enumerate(use)})
            held.append(block)
            tokens_of.append(token)
    hid = activate(own, got, tokens_of)
    other = swap(hid, "pool", 1)
    acc = down_kernel(hid, sel, wt, dw, ds, held, held_at, None)
    acc, send = down_kernel(other, sel, wt, dw, ds, held, held_at, acc)
    for axis, bit in reversed(hops[1:]):
        acc, send = fold(acc, swap(send, axis, bit))
    axis, bit = hops[0]
    return finish(acc, swap(send, axis, bit))


def solution(mesh):
    return jax.shard_map(
        per_device,
        mesh=mesh,
        in_specs=(
            P(("seq", "head"), "pool"),
            P(("seq", "head"), None),
            P(("seq", "head"), None),
            P("seq", "pool", "head"),
            P("seq", "pool", "head"),
            P("seq", "head", "pool"),
            P("seq", "pool", "head"),
            P("seq", "pool", "head"),
            P("seq", "head", "pool"),
        ),
        out_specs=P(("seq", "head"), "pool"),
        check_vma=False,
    )
```

```python
import functools

import jax
import jax.numpy as jnp
from jax import lax
from jax.experimental import pallas as pl
from jax.experimental.pallas import tpu as pltpu
from jax.sharding import PartitionSpec as P

QB = 128
CAP = 2
LANES = 128
BF = jnp.bfloat16
F32 = jnp.float32
I32 = jnp.int32

VM = pl.BlockSpec(memory_space=pltpu.VMEM)
HB = pl.BlockSpec(memory_space=pltpu.HBM)


def sds(shape, dtype):
    return jax.ShapeDtypeStruct(shape, dtype)


def run(kernel, out_shape, in_specs, args, name, limit=2 << 20, flops=0, bytes_=0, **more):
    outs = out_shape if isinstance(out_shape, (list, tuple)) else [out_shape]
    specs = [VM] * len(outs)
    return pl.pallas_call(
        kernel,
        out_shape=out_shape,
        in_specs=in_specs,
        out_specs=specs if isinstance(out_shape, (list, tuple)) else VM,
        compiler_params=pltpu.CompilerParams(vmem_limit_bytes=limit),
        cost_estimate=pl.CostEstimate(flops=flops, bytes_accessed=bytes_, transcendentals=0),
        name=name,
        **more,
    )(*args)


def in_hbm(a):
    return pltpu.with_memory_space_constraint(a, pltpu.HBM)


def in_vmem(a):
    return pltpu.with_memory_space_constraint(a, pltpu.VMEM)


def iota(shape, dim):
    return lax.broadcasted_iota(I32, shape, dim)


def placed(values, start):
    n = values.shape[1]
    spot = (iota((n, LANES), 1) == iota((n, LANES), 0) + start).astype(BF)
    return jnp.dot(values.astype(F32).astype(BF), spot, preferred_element_type=F32)


def pack(tokens, routes, gates):
    rows, width = tokens.shape
    top = routes.shape[1]

    def kernel(t_in, r_in, g_in, x_out, t_v, r_v, g_v, sems):
        copies = [
            pltpu.make_async_copy(src, dst, sems.at[i])
            for i, (src, dst) in enumerate(((r_in, r_v), (g_in, g_v), (t_in, t_v)))
        ]
        for copy in copies:
            copy.start()
        for copy in copies:
            copy.wait()
        x_out[:, :width] = t_v[...]
        gate = g_v[...]
        meta = (
            placed(r_v[...], 0)
            + placed(lax.shift_right_logical(gate, 8), top)
            + placed(gate & 255, 2 * top)
        )
        x_out[:, width:] = meta.astype(BF)

    arrays = [in_hbm(a) for a in (tokens, routes, gates)]
    return run(
        kernel,
        sds((rows, width + LANES), BF),
        [HB] * len(arrays),
        arrays,
        "pack",
        scratch_shapes=[pltpu.VMEM(a.shape, a.dtype) for a in arrays]
        + [pltpu.SemaphoreType.DMA((len(arrays),))],
    )


def cat(a, b, after):
    rows = a.shape[0]

    def kernel(a_ref, b_ref, *rest):
        o_ref = rest[-1]
        o_ref[:rows] = a_ref[...]
        o_ref[rows:] = b_ref[...]

    return run(
        kernel,
        sds((2 * rows,) + a.shape[1:], a.dtype),
        [VM] * (2 + len(after)),
        (a, b, *after),
        "cat",
    )


def moved_bytes(count, rows, columns):
    return 2 * 2 * count * rows * columns


def load(sources, scales, after):
    arrays = []
    for w, _ in sources:
        if not any(w is a for a in arrays):
            arrays.append(w)
    where = [([w is a for a in arrays].index(True), e) for w, e in sources]
    count, n_arrays, n_scales = len(sources), len(arrays), len(scales)
    n_out = 1 if count else 0

    def kernel(*refs):
        w_refs, refs = refs[:n_arrays], refs[n_arrays:]
        s_refs, refs = refs[:n_scales], refs[n_scales + 1 :]
        o_refs, refs = refs[:n_out], refs[n_out:]
        e_refs, refs = refs[:n_scales], refs[n_scales:]
        t_ref, s_v, sems = refs[0], refs[1:-1], refs[-1]
        small = [
            pltpu.make_async_copy(src, dst, sems.at[count + i])
            for i, (src, dst) in enumerate(zip(s_refs, s_v))
        ]
        copies = [
            pltpu.make_async_copy(w_refs[k].at[e], o_refs[0].at[i], sems.at[i])
            for i, (k, e) in enumerate(where)
        ]
        for copy in small + copies:
            copy.start()
        t_ref[...] = jnp.zeros_like(t_ref)
        for copy in small:
            copy.wait()
        for src, dst in zip(s_v, e_refs):
            for a in range(src.shape[0]):
                values = src[a].astype(F32)
                for b in range(src.shape[2]):
                    dst[a, b] = jnp.broadcast_to(values[:, b : b + 1], dst.shape[2:])
        for copy in copies:
            copy.wait()

    spread = [sds((s.shape[0], s.shape[2], s.shape[1], LANES), F32) for s in scales]
    shape = sources[0][0].shape[1:] if count else (0, 0)
    outs = [pltpu.VMEM((count,) + shape, BF)] if count else []
    result = pl.pallas_call(
        kernel,
        out_shape=outs + spread + [sds((8, LANES), F32)],
        in_specs=[HB] * (n_arrays + n_scales) + [VM],
        out_specs=[VM] * (n_out + n_scales + 1),
        scratch_shapes=[pltpu.VMEM(s.shape, s.dtype) for s in scales]
        + [pltpu.SemaphoreType.DMA((count + n_scales,))],
        compiler_params=pltpu.CompilerParams(vmem_limit_bytes=2 << 20),
        cost_estimate=pl.CostEstimate(
            flops=0, bytes_accessed=moved_bytes(count, *shape) + (1 << 20), transcendentals=0
        ),
        name="load",
    )(*[in_hbm(a) for a in arrays + list(scales)], after)
    return result[:n_out], result[n_out:-1], result[-1]


def half_rows(w, other, after):
    experts, hidden, width = w.shape
    n = hidden // 2

    def kernel(w_ref, _, o_ref, t_ref, sems):
        half = lax.rem(lax.axis_index("pool"), 2)
        half = 1 - half if other else half
        cut = pl.ds(pl.multiple_of(half * n, QB), n)
        copies = [
            pltpu.make_async_copy(w_ref.at[e, cut, :], o_ref.at[e], sems.at[e])
            for e in range(experts)
        ]
        for copy in copies:
            copy.start()
        t_ref[...] = jnp.zeros_like(t_ref)
        for copy in copies:
            copy.wait()

    return pl.pallas_call(
        kernel,
        out_shape=[pltpu.VMEM((experts, n, width), BF), sds((8, LANES), F32)],
        in_specs=[HB, VM],
        out_specs=[VM, VM],
        scratch_shapes=[pltpu.SemaphoreType.DMA((experts,))],
        compiler_params=pltpu.CompilerParams(vmem_limit_bytes=1 << 20),
        cost_estimate=pl.CostEstimate(
            flops=0, bytes_accessed=moved_bytes(experts, n, width), transcendentals=0
        ),
        name="half_rows",
    )(in_hbm(w), after)


def dispatch(x, width, top, rows_dev, experts, slots):
    rows = x.shape[0]
    per = slots // experts
    meta = x[:, width:].astype(F32)
    base = (lax.axis_index("seq") * experts).astype(F32)
    lane = iota((rows, LANES), 1)
    named = jnp.where(lane < experts, lane, -LANES).astype(F32) + base
    hits = jnp.zeros((rows, LANES), F32)
    gates = jnp.zeros((rows, LANES), F32)
    total = jnp.zeros((rows, 1), F32)
    for k in range(top):
        gate = meta[:, top + k : top + k + 1] * 256.0 + meta[:, 2 * top + k : 2 * top + k + 1]
        equal = meta[:, k : k + 1] == named
        hits = hits + jnp.where(equal, 1.0, 0.0)
        gates = gates + jnp.where(equal, gate, 0.0)
        total = total + gate
    weights = gates / total
    r0, r1 = iota((rows, rows), 0), iota((rows, rows), 1)
    earlier = ((r0 // rows_dev == r1 // rows_dev) & (r1 < r0)).astype(BF)
    rank = jnp.dot(earlier, hits.astype(BF), preferred_element_type=F32)
    grow = (iota((LANES, slots), 1) // per == iota((LANES, slots), 0)).astype(BF)
    wide_hits = jnp.dot(hits.astype(BF), grow, preferred_element_type=F32)
    wide_rank = jnp.dot(rank.astype(BF), grow, preferred_element_type=F32)
    spot = (iota((rows, slots), 1) % per - (iota((rows, slots), 0) // rows_dev) * CAP).astype(F32)
    sel = jnp.where((wide_hits > 0.5) & (wide_rank == spot), 1.0, 0.0).astype(BF)
    slot_rows = lax.dot_general(
        sel, x[:, :width], (((0,), (0,)), ((), ())), preferred_element_type=F32
    ).astype(BF)
    return sel, weights, slot_rows


def tile(parts):
    return jnp.concatenate([jnp.concatenate(row, axis=1) for row in parts], axis=0)


def scaled(block, scale, a, b, e):
    row = jnp.broadcast_to(scale[a, b, e : e + 1, :], (16, LANES)).astype(BF)
    return (block.reshape(QB // 16, 16, QB) * row[None]).reshape(QB, QB)


def half_products(xs_ref, half, n, place, scales, o_ref, order, before):
    width = xs_ref.shape[1]
    per = xs_ref.shape[0] // len(order)
    columns = [(0, j) for j in range(n)] + [(1, j) for j in range(n)]
    starts = [pl.multiple_of((half * n + j) * QB, QB) for j in range(n)]
    group, deep = 2, 2

    def block(m, e, j, q):
        ref, at, whole = place[m, e]
        cut = pl.ds(starts[j] if whole else j * QB, QB)
        return scaled(ref[at, q * QB : (q + 1) * QB, cut], scales[m], half * n + j, q, e)

    for position, e in enumerate(order):
        before(position)
        xs = xs_ref[e * per : (e + 1) * per, :]
        for at in range(0, len(columns), group):
            acc = jnp.zeros((per, group * QB), F32)
            for d in range(0, width // QB, deep):
                rhs = tile(
                    [[block(m, e, j, q) for m, j in columns[at : at + group]] for q in range(d, d + deep)]
                )
                acc = acc + jnp.dot(
                    xs[:, d * QB : (d + deep) * QB], rhs, preferred_element_type=F32
                )
            o_ref[e * per : (e + 1) * per, at * QB : (at + group) * QB] = acc.astype(o_ref.dtype)


AHEAD = 3


def other_half(x, gw, uw, gs, us, held, held_at, top, rows_dev, block_count):
    experts, width, hidden = gw.shape
    n = hidden // 2 // QB
    slots = experts * block_count * CAP
    rows = block_count * rows_dev
    order = [e for e in range(experts) if (0, e) in held_at]
    kept = len(order)
    order += [e for e in range(experts) if (0, e) not in held_at]
    streamed = [(m, e) for e in order[kept:] for m in (0, 1)]
    count = len(streamed)

    def kernel(x_ref, gw_ref, uw_ref, gs_ref, us_ref, *rest):
        held_refs, rest = rest[: len(held)], rest[len(held) :]
        o_ref, xs_ref, sel_ref, wt_ref, next_ref, buf, sems = rest
        own = lax.rem(lax.axis_index("pool"), 2)

        def copies(half, to, first):
            cut = pl.ds(pl.multiple_of(half * (n * QB), QB), n * QB)
            return [
                pltpu.make_async_copy((gw_ref, uw_ref)[m].at[e, :, cut], to.at[i], sems.at[first + i])
                for i, (m, e) in enumerate(streamed)
            ]

        now, later = copies(1 - own, buf, 0), copies(own, next_ref, count)
        place = {key: (held_refs[ref], at, True) for key, (ref, at) in held_at.items()}
        place.update({key: (buf, i, False) for i, key in enumerate(streamed)})
        due = {}
        for i in range(len(order) - kept):
            due.setdefault(max(-1, kept + i - AHEAD - 1), []).extend(now[2 * i : 2 * i + 2])
        spot = max(-1, len(order) - AHEAD - 1)
        due.setdefault(spot, []).extend(later)

        def before(position):
            for copy in due.get(position, []):
                copy.start()
            i = position - kept
            if i >= 0:
                for copy in now[2 * i : 2 * i + 2]:
                    copy.wait()

        before(-1)
        sel, weights, slot_rows = dispatch(x_ref[...], width, top, rows_dev, experts, slots)
        sel_ref[...] = sel
        wt_ref[...] = weights
        xs_ref[...] = slot_rows
        half_products(xs_ref, 1 - own, n, place, (gs_ref, us_ref), o_ref, order, before)
        for copy in later:
            copy.wait()

    result = run(
        kernel,
        [
            sds((slots, hidden), BF),
            sds((slots, width), BF),
            sds((rows, slots), BF),
            sds((rows, LANES), F32),
            pltpu.VMEM((max(1, count), width, hidden // 2), BF),
        ],
        [VM, HB, HB, VM, VM] + [VM] * len(held),
        (x, in_hbm(gw), in_hbm(uw), gs, us, *[in_vmem(h) for h in held]),
        "other_half",
        limit=16 << 20,
        flops=2 * slots * width * hidden,
        bytes_=2 * experts * width * hidden,
        scratch_shapes=[
            pltpu.VMEM((max(1, count), width, hidden // 2), BF),
            pltpu.SemaphoreType.DMA((max(1, 2 * count),)),
        ],
    )
    return result, {key: i for i, key in enumerate(streamed)}


def own_half(xs, gs, us, dw, held, held_at, half_block, half_at, experts):
    slots, width = xs.shape
    hidden, out_width = dw.shape[1:]
    n = hidden // 2 // QB

    def kernel(xs_ref, gs_ref, us_ref, dw_ref, half_ref, *rest):
        held_refs, (o_ref, d_ref, sems) = rest[: len(held)], rest[len(held) :]
        own = lax.rem(lax.axis_index("pool"), 2)
        cut = pl.ds(pl.multiple_of(own * (n * QB), QB), n * QB)
        copies = [
            pltpu.make_async_copy(dw_ref.at[e, cut, :], d_ref.at[e], sems.at[e])
            for e in range(experts)
        ]
        for copy in copies:
            copy.start()
        place = {key: (held_refs[ref], at, True) for key, (ref, at) in held_at.items()}
        place.update({key: (half_ref, i, False) for key, i in half_at.items()})
        order = list(range(experts))
        half_products(xs_ref, own, n, place, (gs_ref, us_ref), o_ref, order, lambda _: None)
        for copy in copies:
            copy.wait()

    return run(
        kernel,
        [sds((slots, hidden), F32), pltpu.VMEM((experts, hidden // 2, out_width), BF)],
        [VM, VM, VM, HB, VM] + [VM] * len(held),
        (xs, gs, us, in_hbm(dw), in_vmem(half_block), *[in_vmem(h) for h in held]),
        "own_half",
        limit=8 << 20,
        flops=2 * slots * width * hidden,
        bytes_=2 * experts * width * hidden,
        scratch_shapes=[pltpu.SemaphoreType.DMA((experts,))],
    )


def add_round(own, got):
    def kernel(a_ref, b_ref, o_ref, r_ref):
        total = a_ref[...] + b_ref[...].astype(F32)
        o_ref[...] = total
        r_ref[...] = total.astype(BF)

    return run(kernel, [sds(own.shape, F32), sds(own.shape, BF)], [VM] * 2, (own, got), "add_round")


def activate(own, got, after):
    slots, hidden = own.shape
    n = hidden // 2

    def kernel(a_ref, b_ref, *rest):
        o_ref = rest[-1]
        gate = a_ref[:, :n] + b_ref[:, :n].astype(F32)
        up = a_ref[:, n:] + b_ref[:, n:].astype(F32)
        o_ref[...] = (jax.nn.silu(gate) * up).astype(BF)

    return run(
        kernel,
        sds((slots, n), BF),
        [VM] * (2 + len(after)),
        (own, got, *after),
        "activate",
    )


def spread_rows(h_ref, sel_ref, wt_ref, experts):
    rows, slots = sel_ref.shape
    per = slots // experts
    sel = sel_ref[...].astype(F32)
    owner = iota((rows, slots), 1) // per
    stack = jnp.concatenate([jnp.where(owner == e, sel, 0.0) for e in range(experts)], axis=0)
    spread = jnp.dot(stack.astype(BF), h_ref[...], preferred_element_type=F32)
    weights = wt_ref[...]
    return [
        (spread[e * rows : (e + 1) * rows] * weights[:, e : e + 1]).astype(BF)
        for e in range(experts)
    ]


def down_kernel(hid, sel, wt, dw, ds, own):
    experts, half_hidden, width = dw.shape
    n = half_hidden // QB
    rows = sel.shape[0]
    keep = rows // 2
    last = own is not None
    given = [own] if last else []
    group = 2
    pieces = [(e, j) for e in range(experts) for j in range(n)]
    deep = 2 if len(pieces) % 2 == 0 else 1

    def kernel(h_ref, sel_ref, wt_ref, dw_ref, ds_ref, *rest):
        given_refs, outs = rest[: len(given)], rest[len(given) :]
        half = lax.rem(lax.axis_index("pool"), 2)
        half = 1 - half if last else half
        parts = spread_rows(h_ref, sel_ref, wt_ref, experts)

        def block(e, j, q):
            rows_of, columns = slice(j * QB, (j + 1) * QB), slice(q * QB, (q + 1) * QB)
            return scaled(dw_ref[e, rows_of, columns], ds_ref, half * n + j, q, e)

        for c in range(0, width // QB, group):
            at = slice(c * QB, (c + group) * QB)
            acc = given_refs[0][:, at] if last else jnp.zeros((rows, group * QB), F32)
            for p in range(0, len(pieces), deep):
                some = pieces[p : p + deep]
                lhs = jnp.concatenate([parts[e][:, j * QB : (j + 1) * QB] for e, j in some], axis=1)
                rhs = tile([[block(e, j, q) for q in range(c, c + group)] for e, j in some])
                acc = acc + jnp.dot(lhs, rhs, preferred_element_type=F32)
            if last:
                outs[0][:, at] = acc[:keep]
                outs[1][:, at] = acc[keep:].astype(BF)
            else:
                outs[0][:, at] = acc

    return run(
        kernel,
        [sds((keep, width), F32), sds((rows - keep, width), BF)] if last else [sds((rows, width), F32)],
        [VM] * (5 + len(given)),
        (hid, sel, wt, in_vmem(dw), ds, *given),
        "down_other" if last else "down_own",
        limit=8 << 20,
        flops=experts * rows * width * half_hidden * 2,
        bytes_=experts * width * half_hidden * 2,
    )


def fold(own, got):
    rows, width = own.shape
    keep = rows // 2

    def kernel(a_ref, b_ref, o_ref, s_ref):
        o_ref[...] = a_ref[:keep] + b_ref[:keep].astype(F32)
        s_ref[...] = (a_ref[keep:] + b_ref[keep:].astype(F32)).astype(BF)

    return run(
        kernel, [sds((keep, width), F32), sds((keep, width), BF)], [VM] * 2, (own, got), "fold"
    )


def finish(own, got):
    def kernel(a_ref, b_ref, o_ref):
        o_ref[...] = (a_ref[...] + b_ref[...].astype(F32)).astype(BF)

    return run(kernel, sds(own.shape, BF), [VM] * 2, (own, got), "finish")


def swap(x, axis, bit):
    return lax.ppermute(x, axis, [(j, j ^ bit) for j in range(lax.axis_size(axis))])


def bits(count):
    return [1 << i for i in range(count.bit_length() - 1)]


def per_device(tokens, routes, gate_fixed, gw, uw, dw, gs, us, ds):
    n_seq, n_head, n_pool = (lax.axis_size(a) for a in ("seq", "head", "pool"))
    rows_dev, width = tokens.shape
    top = routes.shape[1]
    hops = [("head", b) for b in reversed(bits(n_head))] + [("seq", b) for b in bits(n_seq)]

    experts = gw.shape[0]
    x = pack(tokens, routes, gate_fixed)
    scales = [gs.transpose(2, 0, 1), us.transpose(2, 0, 1), ds.transpose(1, 0, 2)]
    waiting = [(m, e) for e in range(experts * 3 // 8) for m in (0, 1)]
    held, held_at, spread = [], {}, []
    for i, (axis, bit) in enumerate(hops):
        got = swap(x, axis, bit)
        take = -(-len(waiting) // (len(hops) - i))
        after = []
        if take or scales:
            use, waiting = waiting[:take], waiting[take:]
            blocks, rows, token = load([((gw, uw)[m], e) for m, e in use], scales, x)
            held_at.update({key: (len(held), at) for at, key in enumerate(use)})
            held += blocks
            spread += rows
            scales = []
            after = [token]
        x = cat(x, got, after)
    gs, us, ds = spread

    (send, xs, sel, wt, half_block), half_at = other_half(
        x, gw, uw, gs, us, held, held_at, top, rows_dev, n_seq * n_head
    )
    got = swap(send, "pool", 1)
    own, dw_own = own_half(xs, gs, us, dw, held, held_at, half_block, half_at, experts)
    after = []
    for bit in bits(n_pool)[1:]:
        own, send = add_round(own, got)
        got = swap(send, "pool", bit)
        if not after:
            dw_other, token = half_rows(dw, True, send)
            after = [token]
    if not after:
        dw_other, token = half_rows(dw, True, own)
        after = [token]
    hid = activate(own, got, after)
    other = swap(hid, "pool", 1)
    (acc,) = down_kernel(hid, sel, wt, dw_own, ds, None)
    acc, send = down_kernel(other, sel, wt, dw_other, ds, acc)
    for axis, bit in reversed(hops[1:]):
        acc, send = fold(acc, swap(send, axis, bit))
    axis, bit = hops[0]
    return finish(acc, swap(send, axis, bit))


def solution(mesh):
    return jax.shard_map(
        per_device,
        mesh=mesh,
        in_specs=(
            P(("seq", "head"), "pool"),
            P(("seq", "head"), None),
            P(("seq", "head"), None),
            P("seq", "pool", "head"),
            P("seq", "pool", "head"),
            P("seq", "head", "pool"),
            P("seq", "pool", "head"),
            P("seq", "pool", "head"),
            P("seq", "head", "pool"),
        ),
        out_specs=P(("seq", "head"), "pool"),
        check_vma=False,
    )
```

```python
import functools

import jax
import jax.numpy as jnp
from jax import lax
from jax.experimental import pallas as pl
from jax.experimental.pallas import tpu as pltpu
from jax.sharding import PartitionSpec as P

QB = 128
CAP = 2
HINT = 1000
NEAR = 1 << 16
LANES = 128
BF = jnp.bfloat16
F32 = jnp.float32
I32 = jnp.int32

VM = pl.BlockSpec(memory_space=pltpu.VMEM)
HB = pl.BlockSpec(memory_space=pltpu.HBM)


def sds(shape, dtype):
    return jax.ShapeDtypeStruct(shape, dtype)


def run(kernel, out_shape, in_specs, args, name, limit=2 << 20, flops=0, bytes_=0, **more):
    outs = out_shape if isinstance(out_shape, (list, tuple)) else [out_shape]
    specs = [VM] * len(outs)
    return pl.pallas_call(
        kernel,
        out_shape=out_shape,
        in_specs=in_specs,
        out_specs=specs if isinstance(out_shape, (list, tuple)) else VM,
        compiler_params=pltpu.CompilerParams(vmem_limit_bytes=limit),
        cost_estimate=pl.CostEstimate(flops=flops, bytes_accessed=bytes_, transcendentals=0),
        name=name,
        **more,
    )(*args)


def in_hbm(a):
    return pltpu.with_memory_space_constraint(a, pltpu.HBM)


def in_vmem(a):
    return pltpu.with_memory_space_constraint(a, pltpu.VMEM)


def iota(shape, dim):
    return lax.broadcasted_iota(I32, shape, dim)


def placed(values, start):
    n = values.shape[1]
    spot = (iota((n, LANES), 1) == iota((n, LANES), 0) + start).astype(BF)
    return jnp.dot(values.astype(F32).astype(BF), spot, preferred_element_type=F32)


def pack(tokens, routes, gates, hint):
    rows, width = tokens.shape
    top = routes.shape[1]

    def kernel(t_in, r_in, g_in, x_out, t_v, r_v, g_v, sems):
        copies = [
            pltpu.make_async_copy(src, dst, sems.at[i])
            for i, (src, dst) in enumerate(((r_in, r_v), (g_in, g_v), (t_in, t_v)))
        ]
        for copy in copies:
            copy.start()
        for copy in copies:
            copy.wait()
        x_out[:, :width] = t_v[...]
        gate = g_v[...]
        meta = (
            placed(r_v[...], 0)
            + placed(lax.shift_right_logical(gate, 8), top)
            + placed(gate & 255, 2 * top)
        )
        x_out[:, width:] = meta.astype(BF)

    arrays = [in_hbm(a) for a in (tokens, routes, gates)]
    return run(
        kernel,
        sds((rows, width + LANES), BF),
        [HB] * len(arrays),
        arrays,
        "pack",
        flops=hint,
        scratch_shapes=[pltpu.VMEM(a.shape, a.dtype) for a in arrays]
        + [pltpu.SemaphoreType.DMA((len(arrays),))],
    )


def cat(a, b, after):
    rows = a.shape[0]

    def kernel(a_ref, b_ref, *rest):
        o_ref = rest[-1]
        o_ref[:rows] = a_ref[...]
        o_ref[rows:] = b_ref[...]

    return run(
        kernel,
        sds((2 * rows,) + a.shape[1:], a.dtype),
        [VM] * (2 + len(after)),
        (a, b, *after),
        "cat",
    )


def spread_scales(scales, after):
    def kernel(*refs):
        count = len(scales)
        ins, outs, held, sems = refs[:count], refs[count + 1 : 2 * count + 1], refs[2 * count + 1 : -1], refs[-1]
        copies = [
            pltpu.make_async_copy(src, dst, sems.at[i]) for i, (src, dst) in enumerate(zip(ins, held))
        ]
        for copy in copies:
            copy.start()
        for copy, src, dst in zip(copies, held, outs):
            copy.wait()
            for a in range(src.shape[0]):
                values = src[a].astype(F32)
                for b in range(src.shape[2]):
                    dst[a, b] = jnp.broadcast_to(values[:, b : b + 1], dst.shape[2:])

    return run(
        kernel,
        [sds((s.shape[0], s.shape[2], s.shape[1], LANES), F32) for s in scales],
        [HB] * len(scales) + [VM],
        (*[in_hbm(s) for s in scales], after),
        "spread_scales",
        bytes_=1 << 20,
        scratch_shapes=[pltpu.VMEM(s.shape, s.dtype) for s in scales]
        + [pltpu.SemaphoreType.DMA((len(scales),))],
    )


def dispatch(x, width, top, rows_dev, experts, slots):
    rows = x.shape[0]
    per = slots // experts
    meta = x[:, width:].astype(F32)
    base = (lax.axis_index("seq") * experts).astype(F32)
    lane = iota((rows, LANES), 1)
    named = jnp.where(lane < experts, lane, -LANES).astype(F32) + base
    hits = jnp.zeros((rows, LANES), F32)
    gates = jnp.zeros((rows, LANES), F32)
    total = jnp.zeros((rows, 1), F32)
    for k in range(top):
        gate = meta[:, top + k : top + k + 1] * 256.0 + meta[:, 2 * top + k : 2 * top + k + 1]
        equal = meta[:, k : k + 1] == named
        hits = hits + jnp.where(equal, 1.0, 0.0)
        gates = gates + jnp.where(equal, gate, 0.0)
        total = total + gate
    weights = gates / total
    r0, r1 = iota((rows, rows), 0), iota((rows, rows), 1)
    earlier = ((r0 // rows_dev == r1 // rows_dev) & (r1 < r0)).astype(BF)
    rank = jnp.dot(earlier, hits.astype(BF), preferred_element_type=F32)
    grow = (iota((LANES, slots), 1) // per == iota((LANES, slots), 0)).astype(BF)
    wide_hits = jnp.dot(hits.astype(BF), grow, preferred_element_type=F32)
    wide_rank = jnp.dot(rank.astype(BF), grow, preferred_element_type=F32)
    spot = (iota((rows, slots), 1) % per - (iota((rows, slots), 0) // rows_dev) * CAP).astype(F32)
    sel = jnp.where((wide_hits > 0.5) & (wide_rank == spot), 1.0, 0.0).astype(BF)
    slot_rows = lax.dot_general(
        sel, x[:, :width], (((0,), (0,)), ((), ())), preferred_element_type=F32
    ).astype(BF)
    return sel, weights, slot_rows


def tile(parts):
    return jnp.concatenate([jnp.concatenate(row, axis=1) for row in parts], axis=0)


def scaled(block, scale, a, b, e):
    row = jnp.broadcast_to(scale[a, b, e : e + 1, :], (16, LANES)).astype(BF)
    return (block.reshape(QB // 16, 16, QB) * row[None]).reshape(QB, QB)


def half_products(xs_ref, gw, uw, gs, us, o_ref, half):
    experts, width, hidden = gw.shape
    n = hidden // 2 // QB
    per = xs_ref.shape[0] // experts
    columns = [(gw, gs, j) for j in range(n)] + [(uw, us, j) for j in range(n)]
    starts = [pl.multiple_of((half * n + j) * QB, QB) for j in range(n)]
    group, deep = 2, 2

    def block(w, scale, e, j, q):
        part = w[e, q * QB : (q + 1) * QB, pl.ds(starts[j], QB)]
        return scaled(part, scale, half * n + j, q, e)

    for e in range(experts):
        xs = xs_ref[e * per : (e + 1) * per, :]
        for at in range(0, len(columns), group):
            acc = jnp.zeros((per, group * QB), F32)
            for d in range(0, width // QB, deep):
                rhs = tile(
                    [
                        [block(w, s, e, j, q) for w, s, j in columns[at : at + group]]
                        for q in range(d, d + deep)
                    ]
                )
                acc = acc + jnp.dot(
                    xs[:, d * QB : (d + deep) * QB], rhs, preferred_element_type=F32
                )
            o_ref[e * per : (e + 1) * per, at * QB : (at + group) * QB] = acc.astype(o_ref.dtype)


def other_half(x, gw, uw, gs, us, top, rows_dev, block_count):
    experts, width, hidden = gw.shape
    slots = experts * block_count * CAP
    rows = block_count * rows_dev

    def kernel(x_ref, gw_ref, uw_ref, gs_ref, us_ref, o_ref, xs_ref, sel_ref, wt_ref):
        sel, weights, slot_rows = dispatch(x_ref[...], width, top, rows_dev, experts, slots)
        sel_ref[...] = sel
        wt_ref[...] = weights
        xs_ref[...] = slot_rows
        half = 1 - lax.rem(lax.axis_index("pool"), 2)
        half_products(xs_ref, gw_ref, uw_ref, gs_ref, us_ref, o_ref, half)

    return run(
        kernel,
        [
            sds((slots, hidden), BF),
            sds((slots, width), BF),
            sds((rows, slots), BF),
            sds((rows, LANES), F32),
        ],
        [VM] * 5,
        (x, in_vmem(gw), in_vmem(uw), gs, us),
        "other_half",
        limit=8 << 20,
        flops=NEAR,
        bytes_=NEAR,
    )


def own_half(xs, gw, uw, gs, us):
    experts, width, hidden = gw.shape
    slots = xs.shape[0]

    def kernel(xs_ref, gw_ref, uw_ref, gs_ref, us_ref, o_ref):
        half = lax.rem(lax.axis_index("pool"), 2)
        half_products(xs_ref, gw_ref, uw_ref, gs_ref, us_ref, o_ref, half)

    return run(
        kernel,
        sds((slots, hidden), F32),
        [VM] * 5,
        (xs, in_vmem(gw), in_vmem(uw), gs, us),
        "own_half",
        limit=8 << 20,
        flops=NEAR,
        bytes_=NEAR,
    )


def add_round(own, got, hint):
    def kernel(a_ref, b_ref, o_ref, r_ref):
        total = a_ref[...] + b_ref[...].astype(F32)
        o_ref[...] = total
        r_ref[...] = total.astype(BF)

    return run(kernel, [sds(own.shape, F32), sds(own.shape, BF)], [VM] * 2, (own, got), "add_round", flops=hint)


def activate(own, got):
    slots, hidden = own.shape
    n = hidden // 2

    def kernel(a_ref, b_ref, o_ref):
        gate = a_ref[:, :n] + b_ref[:, :n].astype(F32)
        up = a_ref[:, n:] + b_ref[:, n:].astype(F32)
        o_ref[...] = (jax.nn.silu(gate) * up).astype(BF)

    return run(
        kernel,
        sds((slots, n), BF),
        [VM] * 2,
        (own, got),
        "activate",
    )


def spread_rows(h_ref, sel_ref, wt_ref, experts):
    rows, slots = sel_ref.shape
    per = slots // experts
    sel = sel_ref[...].astype(F32)
    owner = iota((rows, slots), 1) // per
    stack = jnp.concatenate([jnp.where(owner == e, sel, 0.0) for e in range(experts)], axis=0)
    spread = jnp.dot(stack.astype(BF), h_ref[...], preferred_element_type=F32)
    weights = wt_ref[...]
    return [
        (spread[e * rows : (e + 1) * rows] * weights[:, e : e + 1]).astype(BF)
        for e in range(experts)
    ]


def down_kernel(hid, sel, wt, dw, ds, own):
    experts, hidden, width = dw.shape
    n = hidden // 2 // QB
    rows = sel.shape[0]
    keep = rows // 2
    last = own is not None
    given = [own] if last else []
    group = 2
    pieces = [(e, j) for e in range(experts) for j in range(n)]
    deep = 2 if len(pieces) % 2 == 0 else 1

    def kernel(h_ref, sel_ref, wt_ref, dw_ref, ds_ref, *rest):
        given_refs, outs = rest[: len(given)], rest[len(given) :]
        half = lax.rem(lax.axis_index("pool"), 2)
        half = 1 - half if last else half
        parts = spread_rows(h_ref, sel_ref, wt_ref, experts)

        starts = [pl.multiple_of((half * n + j) * QB, QB) for j in range(n)]

        def block(e, j, q):
            part = dw_ref[e, pl.ds(starts[j], QB), q * QB : (q + 1) * QB]
            return scaled(part, ds_ref, half * n + j, q, e)

        for c in range(0, width // QB, group):
            at = slice(c * QB, (c + group) * QB)
            acc = given_refs[0][:, at] if last else jnp.zeros((rows, group * QB), F32)
            for p in range(0, len(pieces), deep):
                some = pieces[p : p + deep]
                lhs = jnp.concatenate([parts[e][:, j * QB : (j + 1) * QB] for e, j in some], axis=1)
                rhs = tile([[block(e, j, q) for q in range(c, c + group)] for e, j in some])
                acc = acc + jnp.dot(lhs, rhs, preferred_element_type=F32)
            if last:
                outs[0][:, at] = acc[:keep]
                outs[1][:, at] = acc[keep:].astype(BF)
            else:
                outs[0][:, at] = acc

    return run(
        kernel,
        [sds((keep, width), F32), sds((rows - keep, width), BF)] if last else [sds((rows, width), F32)],
        [VM] * (5 + len(given)),
        (hid, sel, wt, in_vmem(dw), ds, *given),
        "down_other" if last else "down_own",
        limit=8 << 20,
        flops=NEAR,
        bytes_=NEAR,
    )


def fold(own, got):
    rows, width = own.shape
    keep = rows // 2

    def kernel(a_ref, b_ref, o_ref, s_ref):
        o_ref[...] = a_ref[:keep] + b_ref[:keep].astype(F32)
        s_ref[...] = (a_ref[keep:] + b_ref[keep:].astype(F32)).astype(BF)

    return run(
        kernel, [sds((keep, width), F32), sds((keep, width), BF)], [VM] * 2, (own, got), "fold"
    )


def finish(own, got):
    def kernel(a_ref, b_ref, o_ref):
        o_ref[...] = (a_ref[...] + b_ref[...].astype(F32)).astype(BF)

    return run(kernel, sds(own.shape, BF), [VM] * 2, (own, got), "finish")


def swap(x, axis, bit):
    return lax.ppermute(x, axis, [(j, j ^ bit) for j in range(lax.axis_size(axis))])


def bits(count):
    return [1 << i for i in range(count.bit_length() - 1)]


def per_device(tokens, routes, gate_fixed, gw, uw, dw, gs, us, ds):
    n_seq, n_head, n_pool = (lax.axis_size(a) for a in ("seq", "head", "pool"))
    rows_dev, width = tokens.shape
    top = routes.shape[1]
    hops = [("head", b) for b in reversed(bits(n_head))] + [("seq", b) for b in bits(n_seq)]

    x = pack(tokens, routes, gate_fixed, HINT * (gw.size + uw.size))
    scales = [gs.transpose(2, 0, 1), us.transpose(2, 0, 1), ds.transpose(1, 0, 2)]
    for axis, bit in hops:
        got = swap(x, axis, bit)
        if scales:
            gs, us, ds = spread_scales(scales, x)
        x = cat(x, got, [gs] if scales else [])
        scales = []

    send, xs, sel, wt = other_half(x, gw, uw, gs, us, top, rows_dev, n_seq * n_head)
    got = swap(send, "pool", 1)
    own = own_half(xs, gw, uw, gs, us)
    for bit in bits(n_pool)[1:]:
        own, send = add_round(own, got, HINT * dw.size)
        got = swap(send, "pool", bit)
    hid = activate(own, got)
    other = swap(hid, "pool", 1)
    (acc,) = down_kernel(hid, sel, wt, dw, ds, None)
    acc, send = down_kernel(other, sel, wt, dw, ds, acc)
    for axis, bit in reversed(hops[1:]):
        acc, send = fold(acc, swap(send, axis, bit))
    axis, bit = hops[0]
    return finish(acc, swap(send, axis, bit))


def solution(mesh):
    return jax.shard_map(
        per_device,
        mesh=mesh,
        in_specs=(
            P(("seq", "head"), "pool"),
            P(("seq", "head"), None),
            P(("seq", "head"), None),
            P("seq", "pool", "head"),
            P("seq", "pool", "head"),
            P("seq", "head", "pool"),
            P("seq", "pool", "head"),
            P("seq", "pool", "head"),
            P("seq", "head", "pool"),
        ),
        out_specs=P(("seq", "head"), "pool"),
        check_vma=False,
    )
```

```python
import functools

import jax
import jax.numpy as jnp
from jax import lax
from jax.experimental import pallas as pl
from jax.experimental.pallas import tpu as pltpu
from jax.sharding import PartitionSpec as P

QB = 128
CAP = 2
HINT = 1000
NEAR = 1 << 16
LATE = 0
LANES = 128
BF = jnp.bfloat16
F32 = jnp.float32
I32 = jnp.int32

VM = pl.BlockSpec(memory_space=pltpu.VMEM)
HB = pl.BlockSpec(memory_space=pltpu.HBM)


def sds(shape, dtype):
    return jax.ShapeDtypeStruct(shape, dtype)


def run(kernel, out_shape, in_specs, args, name, limit=2 << 20, flops=0, bytes_=0, **more):
    outs = out_shape if isinstance(out_shape, (list, tuple)) else [out_shape]
    specs = [VM] * len(outs)
    return pl.pallas_call(
        kernel,
        out_shape=out_shape,
        in_specs=in_specs,
        out_specs=specs if isinstance(out_shape, (list, tuple)) else VM,
        compiler_params=pltpu.CompilerParams(vmem_limit_bytes=limit),
        cost_estimate=pl.CostEstimate(flops=flops, bytes_accessed=bytes_, transcendentals=0),
        name=name,
        **more,
    )(*args)


def in_hbm(a):
    return pltpu.with_memory_space_constraint(a, pltpu.HBM)


def in_vmem(a):
    return pltpu.with_memory_space_constraint(a, pltpu.VMEM)


def iota(shape, dim):
    return lax.broadcasted_iota(I32, shape, dim)


def placed(values, start):
    n = values.shape[1]
    spot = (iota((n, LANES), 1) == iota((n, LANES), 0) + start).astype(BF)
    return jnp.dot(values.astype(F32).astype(BF), spot, preferred_element_type=F32)


def pack(tokens, routes, gates, hint):
    rows, width = tokens.shape
    top = routes.shape[1]

    def kernel(t_in, r_in, g_in, x_out, t_v, r_v, g_v, sems):
        copies = [
            pltpu.make_async_copy(src, dst, sems.at[i])
            for i, (src, dst) in enumerate(((r_in, r_v), (g_in, g_v), (t_in, t_v)))
        ]
        for copy in copies:
            copy.start()
        for copy in copies:
            copy.wait()
        x_out[:, :width] = t_v[...]
        gate = g_v[...]
        meta = (
            placed(r_v[...], 0)
            + placed(lax.shift_right_logical(gate, 8), top)
            + placed(gate & 255, 2 * top)
        )
        x_out[:, width:] = meta.astype(BF)

    arrays = [in_hbm(a) for a in (tokens, routes, gates)]
    return run(
        kernel,
        sds((rows, width + LANES), BF),
        [HB] * len(arrays),
        arrays,
        "pack",
        flops=hint,
        scratch_shapes=[pltpu.VMEM(a.shape, a.dtype) for a in arrays]
        + [pltpu.SemaphoreType.DMA((len(arrays),))],
    )


def cat(pieces, after, hint=0):
    rows = pieces[0].shape[0]

    def kernel(*refs):
        for i in range(len(pieces)):
            refs[-1][i * rows : (i + 1) * rows] = refs[i][...]

    return run(
        kernel,
        sds((len(pieces) * rows,) + pieces[0].shape[1:], pieces[0].dtype),
        [VM] * (len(pieces) + len(after)),
        (*pieces, *after),
        "cat",
        flops=hint,
    )


def spread_scales(scales, after):
    def kernel(*refs):
        count = len(scales)
        ins, outs, held, sems = refs[:count], refs[count + 1 : 2 * count + 1], refs[2 * count + 1 : -1], refs[-1]
        copies = [
            pltpu.make_async_copy(src, dst, sems.at[i]) for i, (src, dst) in enumerate(zip(ins, held))
        ]
        for copy in copies:
            copy.start()
        for copy, src, dst in zip(copies, held, outs):
            copy.wait()
            for a in range(src.shape[0]):
                values = src[a].astype(F32)
                for b in range(src.shape[2]):
                    dst[a, b] = jnp.broadcast_to(values[:, b : b + 1], dst.shape[2:])

    return run(
        kernel,
        [sds((s.shape[0], s.shape[2], s.shape[1], LANES), F32) for s in scales],
        [HB] * len(scales) + [VM],
        (*[in_hbm(s) for s in scales], after),
        "spread_scales",
        bytes_=1 << 20,
        scratch_shapes=[pltpu.VMEM(s.shape, s.dtype) for s in scales]
        + [pltpu.SemaphoreType.DMA((len(scales),))],
    )


def dispatch(x, width, top, rows_dev, experts, slots):
    rows = x.shape[0]
    per = slots // experts
    meta = x[:, width:].astype(F32)
    base = (lax.axis_index("seq") * experts).astype(F32)
    lane = iota((rows, LANES), 1)
    named = jnp.where(lane < experts, lane, -LANES).astype(F32) + base
    hits = jnp.zeros((rows, LANES), F32)
    gates = jnp.zeros((rows, LANES), F32)
    total = jnp.zeros((rows, 1), F32)
    for k in range(top):
        gate = meta[:, top + k : top + k + 1] * 256.0 + meta[:, 2 * top + k : 2 * top + k + 1]
        equal = meta[:, k : k + 1] == named
        hits = hits + jnp.where(equal, 1.0, 0.0)
        gates = gates + jnp.where(equal, gate, 0.0)
        total = total + gate
    weights = gates / total
    r0, r1 = iota((rows, rows), 0), iota((rows, rows), 1)
    earlier = ((r0 // rows_dev == r1 // rows_dev) & (r1 < r0)).astype(BF)
    rank = jnp.dot(earlier, hits.astype(BF), preferred_element_type=F32)
    grow = (iota((LANES, slots), 1) // per == iota((LANES, slots), 0)).astype(BF)
    wide_hits = jnp.dot(hits.astype(BF), grow, preferred_element_type=F32)
    wide_rank = jnp.dot(rank.astype(BF), grow, preferred_element_type=F32)
    spot = (iota((rows, slots), 1) % per - (iota((rows, slots), 0) // rows_dev) * CAP).astype(F32)
    sel = jnp.where((wide_hits > 0.5) & (wide_rank == spot), 1.0, 0.0).astype(BF)
    slot_rows = lax.dot_general(
        sel, x[:, :width], (((0,), (0,)), ((), ())), preferred_element_type=F32
    ).astype(BF)
    return sel, weights, slot_rows


def tile(parts):
    return jnp.concatenate([jnp.concatenate(row, axis=1) for row in parts], axis=0)


def scaled(block, scale, a, b, e):
    row = jnp.broadcast_to(scale[a, b, e : e + 1, :], (16, LANES)).astype(BF)
    return (block.reshape(QB // 16, 16, QB) * row[None]).reshape(QB, QB)


def half_products(xs_ref, gw, uw, gs, us, o_ref, half):
    experts, width, hidden = gw.shape
    n = hidden // 2 // QB
    per = xs_ref.shape[0] // experts
    columns = [(gw, gs, j) for j in range(n)] + [(uw, us, j) for j in range(n)]
    starts = [pl.multiple_of((half * n + j) * QB, QB) for j in range(n)]
    group, deep = 2, 2

    def block(w, scale, e, j, q):
        part = w[e, q * QB : (q + 1) * QB, pl.ds(starts[j], QB)]
        return scaled(part, scale, half * n + j, q, e)

    for e in range(experts):
        xs = xs_ref[e * per : (e + 1) * per, :]
        for at in range(0, len(columns), group):
            acc = jnp.zeros((per, group * QB), F32)
            for d in range(0, width // QB, deep):
                rhs = tile(
                    [
                        [block(w, s, e, j, q) for w, s, j in columns[at : at + group]]
                        for q in range(d, d + deep)
                    ]
                )
                acc = acc + jnp.dot(
                    xs[:, d * QB : (d + deep) * QB], rhs, preferred_element_type=F32
                )
            o_ref[e * per : (e + 1) * per, at * QB : (at + group) * QB] = acc.astype(o_ref.dtype)


def other_half(x, gw, uw, gs, us, top, rows_dev, block_count):
    experts, width, hidden = gw.shape
    slots = experts * block_count * CAP
    rows = block_count * rows_dev

    def kernel(x_ref, gw_ref, uw_ref, gs_ref, us_ref, o_ref, xs_ref, sel_ref, wt_ref):
        sel, weights, slot_rows = dispatch(x_ref[...], width, top, rows_dev, experts, slots)
        sel_ref[...] = sel
        wt_ref[...] = weights
        xs_ref[...] = slot_rows
        half = 1 - lax.rem(lax.axis_index("pool"), 2)
        half_products(xs_ref, gw_ref, uw_ref, gs_ref, us_ref, o_ref, half)

    return run(
        kernel,
        [
            sds((slots, hidden), BF),
            sds((slots, width), BF),
            sds((rows, slots), BF),
            sds((rows, LANES), F32),
        ],
        [VM] * 5,
        (x, in_vmem(gw), in_vmem(uw), gs, us),
        "other_half",
        limit=8 << 20,
        flops=NEAR,
        bytes_=NEAR,
    )


def own_half(xs, gw, uw, gs, us):
    experts, width, hidden = gw.shape
    slots = xs.shape[0]

    def kernel(xs_ref, gw_ref, uw_ref, gs_ref, us_ref, o_ref):
        half = lax.rem(lax.axis_index("pool"), 2)
        half_products(xs_ref, gw_ref, uw_ref, gs_ref, us_ref, o_ref, half)

    return run(
        kernel,
        sds((slots, hidden), F32),
        [VM] * 5,
        (xs, in_vmem(gw), in_vmem(uw), gs, us),
        "own_half",
        limit=8 << 20,
        flops=NEAR,
        bytes_=NEAR,
    )


def add_round(own, got, hint):
    def kernel(a_ref, b_ref, o_ref, r_ref):
        total = a_ref[...] + b_ref[...].astype(F32)
        o_ref[...] = total
        r_ref[...] = total.astype(BF)

    return run(kernel, [sds(own.shape, F32), sds(own.shape, BF)], [VM] * 2, (own, got), "add_round", flops=hint)


def activate(own, got):
    slots, hidden = own.shape
    n = hidden // 2

    def kernel(a_ref, b_ref, o_ref):
        gate = a_ref[:, :n] + b_ref[:, :n].astype(F32)
        up = a_ref[:, n:] + b_ref[:, n:].astype(F32)
        o_ref[...] = (jax.nn.silu(gate) * up).astype(BF)

    return run(
        kernel,
        sds((slots, n), BF),
        [VM] * 2,
        (own, got),
        "activate",
    )


def spread_rows(h_ref, sel_ref, wt_ref, experts):
    rows, slots = sel_ref.shape
    per = slots // experts
    sel = sel_ref[...].astype(F32)
    owner = iota((rows, slots), 1) // per
    stack = jnp.concatenate([jnp.where(owner == e, sel, 0.0) for e in range(experts)], axis=0)
    spread = jnp.dot(stack.astype(BF), h_ref[...], preferred_element_type=F32)
    weights = wt_ref[...]
    return [
        (spread[e * rows : (e + 1) * rows] * weights[:, e : e + 1]).astype(BF)
        for e in range(experts)
    ]


def down_kernel(hid, sel, wt, dw, ds, own, parts_out):
    experts, hidden, width = dw.shape
    n = hidden // 2 // QB
    rows = sel.shape[0]
    keep = rows // parts_out
    last = own is not None
    given = [own] if last else []
    group = 2
    pieces = [(e, j) for e in range(experts) for j in range(n)]
    deep = 2 if len(pieces) % 2 == 0 else 1

    def kernel(h_ref, sel_ref, wt_ref, dw_ref, ds_ref, *rest):
        given_refs, outs = rest[: len(given)], rest[len(given) :]
        half = lax.rem(lax.axis_index("pool"), 2)
        half = 1 - half if last else half
        parts = spread_rows(h_ref, sel_ref, wt_ref, experts)

        starts = [pl.multiple_of((half * n + j) * QB, QB) for j in range(n)]

        def block(e, j, q):
            part = dw_ref[e, pl.ds(starts[j], QB), q * QB : (q + 1) * QB]
            return scaled(part, ds_ref, half * n + j, q, e)

        for c in range(0, width // QB, group):
            at = slice(c * QB, (c + group) * QB)
            acc = given_refs[0][:, at] if last else jnp.zeros((rows, group * QB), F32)
            for p in range(0, len(pieces), deep):
                some = pieces[p : p + deep]
                lhs = jnp.concatenate([parts[e][:, j * QB : (j + 1) * QB] for e, j in some], axis=1)
                rhs = tile([[block(e, j, q) for q in range(c, c + group)] for e, j in some])
                acc = acc + jnp.dot(lhs, rhs, preferred_element_type=F32)
            if last:
                outs[0][:, at] = acc[:keep]
                for g in range(1, parts_out):
                    outs[g][:, at] = acc[g * keep : (g + 1) * keep].astype(BF)
            else:
                outs[0][:, at] = acc

    return run(
        kernel,
        [sds((keep, width), F32)] + [sds((keep, width), BF)] * (parts_out - 1) if last else [sds((rows, width), F32)],
        [VM] * (5 + len(given)),
        (hid, sel, wt, in_vmem(dw), ds, *given),
        "down_other" if last else "down_own",
        limit=8 << 20,
        flops=NEAR,
        bytes_=NEAR,
    )


def fold(own, got):
    rows, width = own.shape
    keep = rows // 2

    def kernel(a_ref, *rest):
        total = a_ref[...]
        for ref in rest[: len(got)]:
            total = total + ref[...].astype(F32)
        o_ref, s_ref = rest[len(got) :]
        o_ref[...] = total[:keep]
        s_ref[...] = total[keep:].astype(BF)

    return run(
        kernel,
        [sds((keep, width), F32), sds((keep, width), BF)],
        [VM] * (1 + len(got)),
        (own, *got),
        "fold",
    )


def finish(own, got):
    def kernel(a_ref, *rest):
        total = a_ref[...]
        for ref in rest[:-1]:
            total = total + ref[...].astype(F32)
        rest[-1][...] = total.astype(BF)

    return run(kernel, sds(own.shape, BF), [VM] * (1 + len(got)), (own, *got), "finish")


def swap(x, axis, bit):
    return lax.ppermute(x, axis, [(j, j ^ bit) for j in range(lax.axis_size(axis))])


def hop(x, *steps):
    n_seq, n_head = lax.axis_size("seq"), lax.axis_size("head")
    flip = {axis: sum(b for a, b in steps if a == axis) for axis in ("seq", "head")}
    pairs = [
        (s * n_head + h, (s ^ flip["seq"]) * n_head + (h ^ flip["head"]))
        for s in range(n_seq)
        for h in range(n_head)
    ]
    return lax.ppermute(x, ("seq", "head"), pairs)


def bits(count):
    return [1 << i for i in range(count.bit_length() - 1)]


def per_device(tokens, routes, gate_fixed, gw, uw, dw, gs, us, ds):
    n_seq, n_head, n_pool = (lax.axis_size(a) for a in ("seq", "head", "pool"))
    rows_dev, width = tokens.shape
    top = routes.shape[1]
    hops = [("head", b) for b in reversed(bits(n_head))] + [("seq", b) for b in bits(n_seq)]

    x = pack(tokens, routes, gate_fixed, HINT * (gw.size + uw.size))
    scales = [gs.transpose(2, 0, 1), us.transpose(2, 0, 1), ds.transpose(1, 0, 2)]
    single, (a, b) = hops[:-2], hops[-2:]
    for step in single:
        got = hop(x, step)
        if scales:
            gs, us, ds = spread_scales(scales, x)
        x = cat([x, got], [gs] if scales else [], HINT * dw.size * LATE if scales else 0)
        scales = []
    far, near_a, near_b = hop(x, a, b), hop(x, a), hop(x, b)
    x = cat([x, near_a, near_b, far], [])

    send, xs, sel, wt = other_half(x, gw, uw, gs, us, top, rows_dev, n_seq * n_head)
    got = swap(send, "pool", 1)
    own = own_half(xs, gw, uw, gs, us)
    for bit in bits(n_pool)[1:]:
        own, send = add_round(own, got, HINT * dw.size)
        got = swap(send, "pool", bit)
    hid = activate(own, got)
    other = swap(hid, "pool", 1)
    (acc,) = down_kernel(hid, sel, wt, dw, ds, None, 4)
    acc, to_a, to_b, to_far = down_kernel(other, sel, wt, dw, ds, acc, 4)
    far, near_a, near_b = hop(to_far, a, b), hop(to_a, a), hop(to_b, b)
    got = [far, near_b, near_a]
    for step in reversed(single):
        acc, send = fold(acc, got)
        got = [hop(send, step)]
    return finish(acc, got)


def solution(mesh):
    return jax.shard_map(
        per_device,
        mesh=mesh,
        in_specs=(
            P(("seq", "head"), "pool"),
            P(("seq", "head"), None),
            P(("seq", "head"), None),
            P("seq", "pool", "head"),
            P("seq", "pool", "head"),
            P("seq", "head", "pool"),
            P("seq", "pool", "head"),
            P("seq", "pool", "head"),
            P("seq", "head", "pool"),
        ),
        out_specs=P(("seq", "head"), "pool"),
        check_vma=False,
    )
```

```python
import jax
import jax.numpy as jnp
from jax import lax
from jax.experimental import pallas as pl
from jax.experimental.pallas import tpu as pltpu
from jax.sharding import PartitionSpec as P

QB = 128
CAP = 2
HINT = 1000
NEAR = 1 << 16
LATE = 0
LANES = 128
BF = jnp.bfloat16
F32 = jnp.float32
I32 = jnp.int32

VM = pl.BlockSpec(memory_space=pltpu.VMEM)
HB = pl.BlockSpec(memory_space=pltpu.HBM)


def sds(shape, dtype):
    return jax.ShapeDtypeStruct(shape, dtype)


def run(kernel, out_shape, in_specs, args, limit=2 << 20, flops=0, bytes_=0, **more):
    outs = out_shape if isinstance(out_shape, (list, tuple)) else [out_shape]
    specs = [VM] * len(outs)
    return pl.pallas_call(
        kernel,
        out_shape=out_shape,
        in_specs=in_specs,
        out_specs=specs if isinstance(out_shape, (list, tuple)) else VM,
        compiler_params=pltpu.CompilerParams(vmem_limit_bytes=limit),
        cost_estimate=pl.CostEstimate(flops=flops, bytes_accessed=bytes_, transcendentals=0),
        **more,
    )(*args)


def in_hbm(a):
    return pltpu.with_memory_space_constraint(a, pltpu.HBM)


def in_vmem(a):
    return pltpu.with_memory_space_constraint(a, pltpu.VMEM)


def iota(shape, dim):
    return lax.broadcasted_iota(I32, shape, dim)


def placed(values, start):
    n = values.shape[1]
    spot = (iota((n, LANES), 1) == iota((n, LANES), 0) + start).astype(BF)
    return jnp.dot(values.astype(F32).astype(BF), spot, preferred_element_type=F32)


def pack(tokens, routes, gates, hint):
    rows, width = tokens.shape
    top = routes.shape[1]

    def kernel(t_in, r_in, g_in, x_out, t_v, r_v, g_v, sems):
        copies = [
            pltpu.make_async_copy(src, dst, sems.at[i])
            for i, (src, dst) in enumerate(((r_in, r_v), (g_in, g_v), (t_in, t_v)))
        ]
        for copy in copies:
            copy.start()
        for copy in copies:
            copy.wait()
        x_out[:, :width] = t_v[...]
        gate = g_v[...]
        meta = (
            placed(r_v[...], 0)
            + placed(lax.shift_right_logical(gate, 8), top)
            + placed(gate & 255, 2 * top)
        )
        x_out[:, width:] = meta.astype(BF)

    arrays = [in_hbm(a) for a in (tokens, routes, gates)]
    return run(
        kernel,
        sds((rows, width + LANES), BF),
        [HB] * len(arrays),
        arrays,
        flops=hint,
        scratch_shapes=[pltpu.VMEM(a.shape, a.dtype) for a in arrays]
        + [pltpu.SemaphoreType.DMA((len(arrays),))],
    )


def cat(pieces, after, hint=0):
    rows = pieces[0].shape[0]

    def kernel(*refs):
        for i in range(len(pieces)):
            refs[-1][i * rows : (i + 1) * rows] = refs[i][...]

    return run(
        kernel,
        sds((len(pieces) * rows,) + pieces[0].shape[1:], pieces[0].dtype),
        [VM] * (len(pieces) + len(after)),
        (*pieces, *after),
        flops=hint,
    )


def spread_scales(scales, after):
    def kernel(*refs):
        count = len(scales)
        ins, outs, held, sems = refs[:count], refs[count + 1 : 2 * count + 1], refs[2 * count + 1 : -1], refs[-1]
        copies = [
            pltpu.make_async_copy(src, dst, sems.at[i]) for i, (src, dst) in enumerate(zip(ins, held))
        ]
        for copy in copies:
            copy.start()
        for copy, src, dst in zip(copies, held, outs):
            copy.wait()
            for a in range(src.shape[0]):
                values = src[a].astype(F32)
                for b in range(src.shape[2]):
                    dst[a, b] = jnp.broadcast_to(values[:, b : b + 1], dst.shape[2:])

    return run(
        kernel,
        [sds((s.shape[0], s.shape[2], s.shape[1], LANES), F32) for s in scales],
        [HB] * len(scales) + [VM],
        (*[in_hbm(s) for s in scales], after),
        bytes_=1 << 20,
        scratch_shapes=[pltpu.VMEM(s.shape, s.dtype) for s in scales]
        + [pltpu.SemaphoreType.DMA((len(scales),))],
    )


def dispatch(x, width, top, rows_dev, experts, slots):
    rows = x.shape[0]
    per = slots // experts
    meta = x[:, width:].astype(F32)
    base = (lax.axis_index("seq") * experts).astype(F32)
    lane = iota((rows, LANES), 1)
    named = jnp.where(lane < experts, lane, -LANES).astype(F32) + base
    hits = jnp.zeros((rows, LANES), F32)
    gates = jnp.zeros((rows, LANES), F32)
    total = jnp.zeros((rows, 1), F32)
    for k in range(top):
        gate = meta[:, top + k : top + k + 1] * 256.0 + meta[:, 2 * top + k : 2 * top + k + 1]
        equal = meta[:, k : k + 1] == named
        hits = hits + jnp.where(equal, 1.0, 0.0)
        gates = gates + jnp.where(equal, gate, 0.0)
        total = total + gate
    weights = gates / total
    r0, r1 = iota((rows, rows), 0), iota((rows, rows), 1)
    earlier = ((r0 // rows_dev == r1 // rows_dev) & (r1 < r0)).astype(BF)
    rank = jnp.dot(earlier, hits.astype(BF), preferred_element_type=F32)
    grow = (iota((LANES, slots), 1) // per == iota((LANES, slots), 0)).astype(BF)
    wide_hits = jnp.dot(hits.astype(BF), grow, preferred_element_type=F32)
    wide_rank = jnp.dot(rank.astype(BF), grow, preferred_element_type=F32)
    spot = (iota((rows, slots), 1) % per - (iota((rows, slots), 0) // rows_dev) * CAP).astype(F32)
    sel = jnp.where((wide_hits > 0.5) & (wide_rank == spot), 1.0, 0.0).astype(BF)
    slot_rows = lax.dot_general(
        sel, x[:, :width], (((0,), (0,)), ((), ())), preferred_element_type=F32
    ).astype(BF)
    return sel, weights, slot_rows


def tile(parts):
    return jnp.concatenate([jnp.concatenate(row, axis=1) for row in parts], axis=0)


def scaled(block, scale, a, b, e):
    row = jnp.broadcast_to(scale[a, b, e : e + 1, :], (16, LANES)).astype(BF)
    return (block.reshape(QB // 16, 16, QB) * row[None]).reshape(QB, QB)


def half_products(xs_ref, gw, uw, gs, us, o_ref, half, chosen):
    experts, width, hidden = gw.shape
    n = hidden // 2 // QB
    per = xs_ref.shape[0] // experts
    columns = [(gw, gs, j) for j in range(n)] + [(uw, us, j) for j in range(n)]
    starts = [pl.multiple_of((half * n + j) * QB, QB) for j in range(n)]
    group, deep = 2, 2

    def block(w, scale, e, j, q):
        part = w[e, q * QB : (q + 1) * QB, pl.ds(starts[j], QB)]
        return scaled(part, scale, half * n + j, q, e)

    for row, e in enumerate(chosen):
        xs = xs_ref[e * per : (e + 1) * per, :]
        for at in range(0, len(columns), group):
            acc = jnp.zeros((per, group * QB), F32)
            for d in range(0, width // QB, deep):
                rhs = tile(
                    [
                        [block(w, s, e, j, q) for w, s, j in columns[at : at + group]]
                        for q in range(d, d + deep)
                    ]
                )
                acc = acc + jnp.dot(
                    xs[:, d * QB : (d + deep) * QB], rhs, preferred_element_type=F32
                )
            o_ref[row * per : (row + 1) * per, at * QB : (at + group) * QB] = acc.astype(o_ref.dtype)


def other_half(x, gw, uw, gs, us, top, rows_dev, block_count):
    experts, width, hidden = gw.shape
    slots = experts * block_count * CAP
    rows = block_count * rows_dev

    def kernel(x_ref, gw_ref, uw_ref, gs_ref, us_ref, o_ref, xs_ref, sel_ref, wt_ref):
        sel, weights, slot_rows = dispatch(x_ref[...], width, top, rows_dev, experts, slots)
        sel_ref[...] = sel
        wt_ref[...] = weights
        xs_ref[...] = slot_rows
        half = 1 - lax.rem(lax.axis_index("pool"), 2)
        half_products(xs_ref, gw_ref, uw_ref, gs_ref, us_ref, o_ref, half, range(experts))

    return run(
        kernel,
        [
            sds((slots, hidden), BF),
            sds((slots, width), BF),
            sds((rows, slots), BF),
            sds((rows, LANES), F32),
        ],
        [VM] * 5,
        (x, in_vmem(gw), in_vmem(uw), gs, us),
        limit=8 << 20,
        flops=NEAR,
        bytes_=NEAR,
    )


def own_half(xs, gw, uw, gs, us, chosen, after):
    experts, _, hidden = gw.shape
    slots = xs.shape[0] // experts * len(chosen)

    def kernel(xs_ref, gw_ref, uw_ref, gs_ref, us_ref, *rest):
        o_ref = rest[-1]
        half = lax.rem(lax.axis_index("pool"), 2)
        half_products(xs_ref, gw_ref, uw_ref, gs_ref, us_ref, o_ref, half, chosen)

    return run(
        kernel,
        sds((slots, hidden), F32),
        [VM] * (5 + len(after)),
        (xs, in_vmem(gw), in_vmem(uw), gs, us, *after),
        limit=8 << 20,
        flops=NEAR,
        bytes_=NEAR,
    )


def add_round(own, got, first, hint):
    rows = own.shape[0]

    def kernel(a_ref, b_ref, o_ref, r_ref):
        total = a_ref[...] + b_ref[first : first + rows].astype(F32)
        o_ref[...] = total
        r_ref[...] = total.astype(BF)

    return run(kernel, [sds(own.shape, F32), sds(own.shape, BF)], [VM] * 2, (own, got), flops=hint)


def activate(own, got, after):
    slots, hidden = own.shape
    n = hidden // 2

    def kernel(a_ref, b_ref, *rest):
        o_ref = rest[-1]
        gate = a_ref[:, :n] + b_ref[:, :n].astype(F32)
        up = a_ref[:, n:] + b_ref[:, n:].astype(F32)
        o_ref[...] = (jax.nn.silu(gate) * up).astype(BF)

    return run(kernel, sds((slots, n), BF), [VM] * (2 + len(after)), (own, got, *after))


def spread_rows(h_ref, sel_ref, wt_ref, per, chosen):
    rows = sel_ref.shape[0]
    low = chosen[0] * per
    slots = h_ref.shape[0]
    sel = sel_ref[:, low : low + slots].astype(F32)
    owner = iota((rows, slots), 1) // per
    stack = jnp.concatenate(
        [jnp.where(owner == i, sel, 0.0) for i in range(len(chosen))], axis=0
    )
    spread = jnp.dot(stack.astype(BF), h_ref[...], preferred_element_type=F32)
    weights = wt_ref[...]
    return {
        e: (spread[i * rows : (i + 1) * rows] * weights[:, e : e + 1]).astype(BF)
        for i, e in enumerate(chosen)
    }


def down_kernel(hid, sel, wt, dw, ds, acc_in, chosen, other, parts_out):
    experts, hidden, width = dw.shape
    n = hidden // 2 // QB
    rows, slots = sel.shape
    per = slots // experts
    keep = rows // parts_out
    last = parts_out > 1
    given = [] if acc_in is None else [acc_in]
    group = 2
    pieces = [(e, j) for e in chosen for j in range(n)]
    deep = 2 if len(pieces) % 2 == 0 else 1

    def kernel(h_ref, sel_ref, wt_ref, dw_ref, ds_ref, *rest):
        given_refs, outs = rest[: len(given)], rest[len(given) :]
        half = lax.rem(lax.axis_index("pool"), 2)
        half = 1 - half if other else half
        parts = spread_rows(h_ref, sel_ref, wt_ref, per, chosen)
        starts = [pl.multiple_of((half * n + j) * QB, QB) for j in range(n)]

        def block(e, j, q):
            part = dw_ref[e, pl.ds(starts[j], QB), q * QB : (q + 1) * QB]
            return scaled(part, ds_ref, half * n + j, q, e)

        for c in range(0, width // QB, group):
            at = slice(c * QB, (c + group) * QB)
            acc = given_refs[0][:, at] if given else jnp.zeros((rows, group * QB), F32)
            for p in range(0, len(pieces), deep):
                some = pieces[p : p + deep]
                lhs = jnp.concatenate([parts[e][:, j * QB : (j + 1) * QB] for e, j in some], axis=1)
                rhs = tile([[block(e, j, q) for q in range(c, c + group)] for e, j in some])
                acc = acc + jnp.dot(lhs, rhs, preferred_element_type=F32)
            if last:
                outs[0][:, at] = acc[:keep]
                for g in range(1, parts_out):
                    outs[g][:, at] = acc[g * keep : (g + 1) * keep].astype(BF)
            else:
                outs[0][:, at] = acc

    return run(
        kernel,
        [sds((keep, width), F32)] + [sds((keep, width), BF)] * (parts_out - 1),
        [VM] * (5 + len(given)),
        (hid, sel, wt, in_vmem(dw), ds, *given),
        limit=8 << 20,
        flops=NEAR,
        bytes_=NEAR,
    )


def fold(own, got):
    rows, width = own.shape
    keep = rows // 2

    def kernel(a_ref, *rest):
        total = a_ref[...]
        for ref in rest[: len(got)]:
            total = total + ref[...].astype(F32)
        o_ref, s_ref = rest[len(got) :]
        o_ref[...] = total[:keep]
        s_ref[...] = total[keep:].astype(BF)

    return run(
        kernel,
        [sds((keep, width), F32), sds((keep, width), BF)],
        [VM] * (1 + len(got)),
        (own, *got),
    )


def finish(own, got):
    def kernel(a_ref, *rest):
        total = a_ref[...]
        for ref in rest[:-1]:
            total = total + ref[...].astype(F32)
        rest[-1][...] = total.astype(BF)

    return run(kernel, sds(own.shape, BF), [VM] * (1 + len(got)), (own, *got))


def swap(x, axis, bit):
    return lax.ppermute(x, axis, [(j, j ^ bit) for j in range(lax.axis_size(axis))])


def hop(x, *steps):
    n_seq, n_head = lax.axis_size("seq"), lax.axis_size("head")
    flip = {axis: sum(b for a, b in steps if a == axis) for axis in ("seq", "head")}
    pairs = [
        (s * n_head + h, (s ^ flip["seq"]) * n_head + (h ^ flip["head"]))
        for s in range(n_seq)
        for h in range(n_head)
    ]
    return lax.ppermute(x, ("seq", "head"), pairs)


def bits(count):
    return [1 << i for i in range(count.bit_length() - 1)]


def per_device(tokens, routes, gate_fixed, gw, uw, dw, gs, us, ds):
    n_seq, n_head, n_pool = (lax.axis_size(a) for a in ("seq", "head", "pool"))
    rows_dev, _ = tokens.shape
    top = routes.shape[1]
    hops = [("head", b) for b in reversed(bits(n_head))] + [("seq", b) for b in bits(n_seq)]

    x = pack(tokens, routes, gate_fixed, HINT * (gw.size + uw.size))
    scales = [gs.transpose(2, 0, 1), us.transpose(2, 0, 1), ds.transpose(1, 0, 2)]
    single, (a, b) = hops[:-2], hops[-2:]
    for step in single:
        got = hop(x, step)
        if scales:
            gs, us, ds = spread_scales(scales, x)
        x = cat([x, got], [gs] if scales else [], HINT * dw.size * LATE if scales else 0)
        scales = []
    far, near_a, near_b = hop(x, a, b), hop(x, a), hop(x, b)
    x = cat([x, near_a, near_b, far], [])

    send, xs, sel, wt = other_half(x, gw, uw, gs, us, top, rows_dev, n_seq * n_head)
    got = swap(send, "pool", 1)
    experts = gw.shape[0]
    per = xs.shape[0] // experts
    cut = experts // 2
    parts = [range(cut), range(cut, experts)] if cut else [range(experts)]
    steps = bits(n_pool)[1:]
    sums, after = [], []
    for i, part in enumerate(parts):
        own = own_half(xs, gw, uw, gs, us, part, after)
        first, hint = part[0] * per, HINT * dw.size
        arrived = got
        for bit in steps:
            own, send = add_round(own, arrived, first, hint if i + 1 == len(parts) else 0)
            arrived, first = swap(send, "pool", bit), 0
            after = [send]
        sums.append((own, arrived))
    acc = None
    for i, (part, pair) in enumerate(zip(parts, sums)):
        hid = activate(*pair, [] if acc is None else [acc])
        other = swap(hid, "pool", 1)
        (acc,) = down_kernel(hid, sel, wt, dw, ds, acc, part, False, 1)
        ends = i + 1 == len(parts)
        acc, *sends = down_kernel(other, sel, wt, dw, ds, acc, part, True, 4 if ends else 1)
    to_a, to_b, to_far = sends
    far, near_a, near_b = hop(to_far, a, b), hop(to_a, a), hop(to_b, b)
    got = [far, near_b, near_a]
    for step in reversed(single):
        acc, send = fold(acc, got)
        got = [hop(send, step)]
    return finish(acc, got)


def solution(mesh):
    return jax.shard_map(
        per_device,
        mesh=mesh,
        in_specs=(
            P(("seq", "head"), "pool"),
            P(("seq", "head"), None),
            P(("seq", "head"), None),
            P("seq", "pool", "head"),
            P("seq", "pool", "head"),
            P("seq", "head", "pool"),
            P("seq", "pool", "head"),
            P("seq", "pool", "head"),
            P("seq", "head", "pool"),
        ),
        out_specs=P(("seq", "head"), "pool"),
        check_vma=False,
    )
```

```python
import jax
import jax.numpy as jnp
from jax import lax
from jax.experimental import pallas as pl
from jax.experimental.pallas import tpu as pltpu
from jax.sharding import PartitionSpec as P

QB = 128
CAP = 2
HINT = 1000
NEAR = 1 << 16
LATE = 0
LANES = 128
BF = jnp.bfloat16
F32 = jnp.float32
I32 = jnp.int32

VM = pl.BlockSpec(memory_space=pltpu.VMEM)
HB = pl.BlockSpec(memory_space=pltpu.HBM)


def sds(shape, dtype):
    return jax.ShapeDtypeStruct(shape, dtype)


def run(kernel, out_shape, in_specs, args, limit=2 << 20, flops=0, bytes_=0, **more):
    outs = out_shape if isinstance(out_shape, (list, tuple)) else [out_shape]
    specs = [VM] * len(outs)
    return pl.pallas_call(
        kernel,
        out_shape=out_shape,
        in_specs=in_specs,
        out_specs=specs if isinstance(out_shape, (list, tuple)) else VM,
        compiler_params=pltpu.CompilerParams(vmem_limit_bytes=limit),
        cost_estimate=pl.CostEstimate(flops=flops, bytes_accessed=bytes_, transcendentals=0),
        **more,
    )(*args)


def in_hbm(a):
    return pltpu.with_memory_space_constraint(a, pltpu.HBM)


def in_vmem(a):
    return pltpu.with_memory_space_constraint(a, pltpu.VMEM)


def iota(shape, dim):
    return lax.broadcasted_iota(I32, shape, dim)


def placed(values, start):
    n = values.shape[1]
    spot = (iota((n, LANES), 1) == iota((n, LANES), 0) + start).astype(BF)
    return jnp.dot(values.astype(F32).astype(BF), spot, preferred_element_type=F32)


def pack(tokens, routes, gates, hint):
    rows, width = tokens.shape
    top = routes.shape[1]

    def kernel(t_in, r_in, g_in, x_out, t_v, r_v, g_v, sems):
        copies = [
            pltpu.make_async_copy(src, dst, sems.at[i])
            for i, (src, dst) in enumerate(((r_in, r_v), (g_in, g_v), (t_in, t_v)))
        ]
        for copy in copies:
            copy.start()
        for copy in copies:
            copy.wait()
        x_out[:, :width] = t_v[...]
        gate = g_v[...]
        meta = (
            placed(r_v[...], 0)
            + placed(lax.shift_right_logical(gate, 8), top)
            + placed(gate & 255, 2 * top)
        )
        x_out[:, width:] = meta.astype(BF)

    arrays = [in_hbm(a) for a in (tokens, routes, gates)]
    return run(
        kernel,
        sds((rows, width + LANES), BF),
        [HB] * len(arrays),
        arrays,
        flops=hint,
        scratch_shapes=[pltpu.VMEM(a.shape, a.dtype) for a in arrays]
        + [pltpu.SemaphoreType.DMA((len(arrays),))],
    )


def cat(pieces, after, hint=0):
    rows = pieces[0].shape[0]

    def kernel(*refs):
        for i in range(len(pieces)):
            refs[-1][i * rows : (i + 1) * rows] = refs[i][...]

    return run(
        kernel,
        sds((len(pieces) * rows,) + pieces[0].shape[1:], pieces[0].dtype),
        [VM] * (len(pieces) + len(after)),
        (*pieces, *after),
        flops=hint,
    )


def spread_scales(scales, after):
    def kernel(*refs):
        count = len(scales)
        ins, outs, held, sems = refs[:count], refs[count + 1 : 2 * count + 1], refs[2 * count + 1 : -1], refs[-1]
        copies = [
            pltpu.make_async_copy(src, dst, sems.at[i]) for i, (src, dst) in enumerate(zip(ins, held))
        ]
        for copy in copies:
            copy.start()
        for copy, src, dst in zip(copies, held, outs):
            copy.wait()
            for a in range(src.shape[0]):
                values = src[a].astype(F32)
                for b in range(src.shape[2]):
                    dst[a, b] = jnp.broadcast_to(values[:, b : b + 1], dst.shape[2:])

    return run(
        kernel,
        [sds((s.shape[0], s.shape[2], s.shape[1], LANES), F32) for s in scales],
        [HB] * len(scales) + [VM],
        (*[in_hbm(s) for s in scales], after),
        bytes_=1 << 20,
        scratch_shapes=[pltpu.VMEM(s.shape, s.dtype) for s in scales]
        + [pltpu.SemaphoreType.DMA((len(scales),))],
    )


def half_rows(w, other, after):
    experts, hidden, width = w.shape
    n = hidden // 2

    def kernel(w_ref, _, o_ref, t_ref, sems):
        half = lax.rem(lax.axis_index("pool"), 2)
        half = 1 - half if other else half
        cut = pl.ds(pl.multiple_of(half * n, QB), n)
        copies = [
            pltpu.make_async_copy(w_ref.at[e, cut, :], o_ref.at[e], sems.at[e])
            for e in range(experts)
        ]
        for copy in copies:
            copy.start()
        t_ref[...] = jnp.zeros_like(t_ref)
        for copy in copies:
            copy.wait()

    return pl.pallas_call(
        kernel,
        out_shape=[pltpu.VMEM((experts, n, width), BF), sds((8, LANES), F32)],
        in_specs=[HB, VM],
        out_specs=[VM, VM],
        scratch_shapes=[pltpu.SemaphoreType.DMA((experts,))],
        compiler_params=pltpu.CompilerParams(vmem_limit_bytes=1 << 20),
        cost_estimate=pl.CostEstimate(
            flops=NEAR, bytes_accessed=NEAR, transcendentals=0
        ),
        name="half_rows",
    )(in_hbm(w), after)


def dispatch(x, width, top, rows_dev, experts, slots):
    rows = x.shape[0]
    per = slots // experts
    meta = x[:, width:].astype(F32)
    base = (lax.axis_index("seq") * experts).astype(F32)
    lane = iota((rows, LANES), 1)
    named = jnp.where(lane < experts, lane, -LANES).astype(F32) + base
    hits = jnp.zeros((rows, LANES), F32)
    gates = jnp.zeros((rows, LANES), F32)
    total = jnp.zeros((rows, 1), F32)
    for k in range(top):
        gate = meta[:, top + k : top + k + 1] * 256.0 + meta[:, 2 * top + k : 2 * top + k + 1]
        equal = meta[:, k : k + 1] == named
        hits = hits + jnp.where(equal, 1.0, 0.0)
        gates = gates + jnp.where(equal, gate, 0.0)
        total = total + gate
    weights = gates / total
    r0, r1 = iota((rows, rows), 0), iota((rows, rows), 1)
    earlier = ((r0 // rows_dev == r1 // rows_dev) & (r1 < r0)).astype(BF)
    rank = jnp.dot(earlier, hits.astype(BF), preferred_element_type=F32)
    grow = (iota((LANES, slots), 1) // per == iota((LANES, slots), 0)).astype(BF)
    wide_hits = jnp.dot(hits.astype(BF), grow, preferred_element_type=F32)
    wide_rank = jnp.dot(rank.astype(BF), grow, preferred_element_type=F32)
    spot = (iota((rows, slots), 1) % per - (iota((rows, slots), 0) // rows_dev) * CAP).astype(F32)
    sel = jnp.where((wide_hits > 0.5) & (wide_rank == spot), 1.0, 0.0).astype(BF)
    slot_rows = lax.dot_general(
        sel, x[:, :width], (((0,), (0,)), ((), ())), preferred_element_type=F32
    ).astype(BF)
    return sel, weights, slot_rows


def tile(parts):
    return jnp.concatenate([jnp.concatenate(row, axis=1) for row in parts], axis=0)


def scaled(block, scale, a, b, e):
    row = jnp.broadcast_to(scale[a, b, e : e + 1, :], (16, LANES)).astype(BF)
    return (block.reshape(QB // 16, 16, QB) * row[None]).reshape(QB, QB)


def half_products(xs_ref, gw, uw, gs, us, o_ref, half, chosen):
    experts, width, hidden = gw.shape
    n = hidden // 2 // QB
    per = xs_ref.shape[0] // experts
    columns = [(gw, gs, j) for j in range(n)] + [(uw, us, j) for j in range(n)]
    starts = [pl.multiple_of((half * n + j) * QB, QB) for j in range(n)]
    group, deep = 2, 2

    def block(w, scale, e, j, q):
        part = w[e, q * QB : (q + 1) * QB, pl.ds(starts[j], QB)]
        return scaled(part, scale, half * n + j, q, e)

    for row, e in enumerate(chosen):
        xs = xs_ref[e * per : (e + 1) * per, :]
        for at in range(0, len(columns), group):
            acc = jnp.zeros((per, group * QB), F32)
            for d in range(0, width // QB, deep):
                rhs = tile(
                    [
                        [block(w, s, e, j, q) for w, s, j in columns[at : at + group]]
                        for q in range(d, d + deep)
                    ]
                )
                acc = acc + jnp.dot(
                    xs[:, d * QB : (d + deep) * QB], rhs, preferred_element_type=F32
                )
            o_ref[row * per : (row + 1) * per, at * QB : (at + group) * QB] = acc.astype(o_ref.dtype)


def other_half(x, gw, uw, gs, us, top, rows_dev, block_count):
    experts, width, hidden = gw.shape
    slots = experts * block_count * CAP
    rows = block_count * rows_dev

    def kernel(x_ref, gw_ref, uw_ref, gs_ref, us_ref, o_ref, xs_ref, sel_ref, wt_ref):
        sel, weights, slot_rows = dispatch(x_ref[...], width, top, rows_dev, experts, slots)
        sel_ref[...] = sel
        wt_ref[...] = weights
        xs_ref[...] = slot_rows
        half = 1 - lax.rem(lax.axis_index("pool"), 2)
        half_products(xs_ref, gw_ref, uw_ref, gs_ref, us_ref, o_ref, half, range(experts))

    return run(
        kernel,
        [
            sds((slots, hidden), BF),
            sds((slots, width), BF),
            sds((rows, slots), BF),
            sds((rows, LANES), F32),
        ],
        [VM] * 5,
        (x, in_vmem(gw), in_vmem(uw), gs, us),
        limit=8 << 20,
        flops=NEAR,
        bytes_=NEAR,
    )


def own_half(xs, gw, uw, gs, us, chosen, after):
    experts, _, hidden = gw.shape
    slots = xs.shape[0] // experts * len(chosen)

    def kernel(xs_ref, gw_ref, uw_ref, gs_ref, us_ref, *rest):
        o_ref = rest[-1]
        half = lax.rem(lax.axis_index("pool"), 2)
        half_products(xs_ref, gw_ref, uw_ref, gs_ref, us_ref, o_ref, half, chosen)

    return run(
        kernel,
        sds((slots, hidden), F32),
        [VM] * (5 + len(after)),
        (xs, in_vmem(gw), in_vmem(uw), gs, us, *after),
        limit=8 << 20,
        flops=NEAR,
        bytes_=NEAR,
    )


def add_round(own, got, first):
    rows = own.shape[0]

    def kernel(a_ref, b_ref, o_ref, r_ref):
        total = a_ref[...] + b_ref[first : first + rows].astype(F32)
        o_ref[...] = total
        r_ref[...] = total.astype(BF)

    return run(kernel, [sds(own.shape, F32), sds(own.shape, BF)], [VM] * 2, (own, got))


def activate(pairs, after):
    hidden = pairs[0][0].shape[1]
    rows = [own.shape[0] for own, _ in pairs]
    n = hidden // 2

    def kernel(*refs):
        first = 0
        for i, count in enumerate(rows):
            a_ref, b_ref = refs[2 * i : 2 * i + 2]
            gate = a_ref[:, :n] + b_ref[:, :n].astype(F32)
            up = a_ref[:, n:] + b_ref[:, n:].astype(F32)
            refs[-1][first : first + count] = (jax.nn.silu(gate) * up).astype(BF)
            first += count

    return run(
        kernel,
        sds((sum(rows), n), BF),
        [VM] * (2 * len(pairs) + 1),
        [a for pair in pairs for a in pair] + [after],
    )


def spread_rows(h_ref, sel_ref, wt_ref, per, chosen):
    rows = sel_ref.shape[0]
    low = chosen[0] * per
    slots = h_ref.shape[0]
    sel = sel_ref[:, low : low + slots].astype(F32)
    owner = iota((rows, slots), 1) // per
    stack = jnp.concatenate(
        [jnp.where(owner == i, sel, 0.0) for i in range(len(chosen))], axis=0
    )
    spread = jnp.dot(stack.astype(BF), h_ref[...], preferred_element_type=F32)
    weights = wt_ref[...]
    return {
        e: (spread[i * rows : (i + 1) * rows] * weights[:, e : e + 1]).astype(BF)
        for i, e in enumerate(chosen)
    }


def down_kernel(hid, sel, wt, dw, ds, acc_in, chosen, other, parts_out):
    experts, half_hidden, width = dw.shape
    n = half_hidden // QB
    rows, slots = sel.shape
    per = slots // experts
    keep = rows // parts_out
    last = parts_out > 1
    given = [] if acc_in is None else [acc_in]
    group = 2
    pieces = [(e, j) for e in chosen for j in range(n)]
    deep = 2 if len(pieces) % 2 == 0 else 1

    def kernel(h_ref, sel_ref, wt_ref, dw_ref, ds_ref, *rest):
        given_refs, outs = rest[: len(given)], rest[len(given) :]
        half = lax.rem(lax.axis_index("pool"), 2)
        half = 1 - half if other else half
        parts = spread_rows(h_ref, sel_ref, wt_ref, per, chosen)

        def block(e, j, q):
            part = dw_ref[e, j * QB : (j + 1) * QB, q * QB : (q + 1) * QB]
            return scaled(part, ds_ref, half * n + j, q, e)

        for c in range(0, width // QB, group):
            at = slice(c * QB, (c + group) * QB)
            acc = given_refs[0][:, at] if given else jnp.zeros((rows, group * QB), F32)
            for p in range(0, len(pieces), deep):
                some = pieces[p : p + deep]
                lhs = jnp.concatenate([parts[e][:, j * QB : (j + 1) * QB] for e, j in some], axis=1)
                rhs = tile([[block(e, j, q) for q in range(c, c + group)] for e, j in some])
                acc = acc + jnp.dot(lhs, rhs, preferred_element_type=F32)
            if last:
                outs[0][:, at] = acc[:keep]
                for g in range(1, parts_out):
                    outs[g][:, at] = acc[g * keep : (g + 1) * keep].astype(BF)
            else:
                outs[0][:, at] = acc

    return run(
        kernel,
        [sds((keep, width), F32)] + [sds((keep, width), BF)] * (parts_out - 1),
        [VM] * (5 + len(given)),
        (hid, sel, wt, in_vmem(dw), ds, *given),
        limit=8 << 20,
        flops=NEAR,
        bytes_=NEAR,
    )


def fold(own, got):
    rows, width = own.shape
    keep = rows // 2

    def kernel(a_ref, *rest):
        total = a_ref[...]
        for ref in rest[: len(got)]:
            total = total + ref[...].astype(F32)
        o_ref, s_ref = rest[len(got) :]
        o_ref[...] = total[:keep]
        s_ref[...] = total[keep:].astype(BF)

    return run(
        kernel,
        [sds((keep, width), F32), sds((keep, width), BF)],
        [VM] * (1 + len(got)),
        (own, *got),
    )


def finish(own, got):
    def kernel(a_ref, *rest):
        total = a_ref[...]
        for ref in rest[:-1]:
            total = total + ref[...].astype(F32)
        rest[-1][...] = total.astype(BF)

    return run(kernel, sds(own.shape, BF), [VM] * (1 + len(got)), (own, *got))


def swap(x, axis, bit):
    return lax.ppermute(x, axis, [(j, j ^ bit) for j in range(lax.axis_size(axis))])


def hop(x, *steps):
    n_seq, n_head = lax.axis_size("seq"), lax.axis_size("head")
    flip = {axis: sum(b for a, b in steps if a == axis) for axis in ("seq", "head")}
    pairs = [
        (s * n_head + h, (s ^ flip["seq"]) * n_head + (h ^ flip["head"]))
        for s in range(n_seq)
        for h in range(n_head)
    ]
    return lax.ppermute(x, ("seq", "head"), pairs)


def bits(count):
    return [1 << i for i in range(count.bit_length() - 1)]


def per_device(tokens, routes, gate_fixed, gw, uw, dw, gs, us, ds):
    n_seq, n_head, n_pool = (lax.axis_size(a) for a in ("seq", "head", "pool"))
    rows_dev, _ = tokens.shape
    top = routes.shape[1]
    hops = [("head", b) for b in reversed(bits(n_head))] + [("seq", b) for b in bits(n_seq)]

    x = pack(tokens, routes, gate_fixed, HINT * (gw.size + uw.size))
    scales = [gs.transpose(2, 0, 1), us.transpose(2, 0, 1), ds.transpose(1, 0, 2)]
    single, (a, b) = hops[:-2], hops[-2:]
    for step in single:
        got = hop(x, step)
        if scales:
            gs, us, ds = spread_scales(scales, x)
        x = cat([x, got], [gs] if scales else [], HINT * dw.size * LATE if scales else 0)
        scales = []
    far, near_b = hop(x, a, b), hop(x, b)
    near_a = hop(x, a)
    dw_own, token = half_rows(dw, False, x)
    x = cat([x, near_a, near_b, far], [token])

    send, xs, sel, wt = other_half(x, gw, uw, gs, us, top, rows_dev, n_seq * n_head)
    got = swap(send, "pool", 1)
    experts = gw.shape[0]
    per = xs.shape[0] // experts
    cut = experts * 5 // 8
    parts = [range(cut), range(cut, experts)] if cut else [range(experts)]
    steps = bits(n_pool)[1:]
    sums, after = [], []
    for part in parts:
        own = own_half(xs, gw, uw, gs, us, part, after)
        first = part[0] * per
        arrived = got
        for bit in steps:
            own, send = add_round(own, arrived, first)
            arrived, first = swap(send, "pool", bit), 0
            after = [send]
        sums.append((own, arrived))
    everyone = range(experts)
    dw_other, token = half_rows(dw, True, sums[-1][0])
    hid = activate(sums, token)
    other = swap(hid, "pool", 1)
    (acc,) = down_kernel(hid, sel, wt, dw_own, ds, None, everyone, False, 1)
    acc, to_a, to_b, to_far = down_kernel(other, sel, wt, dw_other, ds, acc, everyone, True, 4)
    far, near_a, near_b = hop(to_far, a, b), hop(to_a, a), hop(to_b, b)
    got = [far, near_b, near_a]
    for step in reversed(single):
        acc, send = fold(acc, got)
        got = [hop(send, step)]
    return finish(acc, got)


def solution(mesh):
    return jax.shard_map(
        per_device,
        mesh=mesh,
        in_specs=(
            P(("seq", "head"), "pool"),
            P(("seq", "head"), None),
            P(("seq", "head"), None),
            P("seq", "pool", "head"),
            P("seq", "pool", "head"),
            P("seq", "head", "pool"),
            P("seq", "pool", "head"),
            P("seq", "pool", "head"),
            P("seq", "head", "pool"),
        ),
        out_specs=P(("seq", "head"), "pool"),
        check_vma=False,
    )
```

```python
import jax
import jax.numpy as jnp
from jax import lax
from jax.experimental import pallas as pl
from jax.experimental.pallas import tpu as pltpu
from jax.sharding import PartitionSpec as P

QB = 128
CAP = 2
HINT = 1000
NEAR = 1 << 16
LATE = 0
LANES = 128
BF = jnp.bfloat16
F32 = jnp.float32
I32 = jnp.int32

VM = pl.BlockSpec(memory_space=pltpu.VMEM)
HB = pl.BlockSpec(memory_space=pltpu.HBM)


def sds(shape, dtype):
    return jax.ShapeDtypeStruct(shape, dtype)


def run(kernel, out_shape, in_specs, args, limit=2 << 20, flops=0, bytes_=0, **more):
    outs = out_shape if isinstance(out_shape, (list, tuple)) else [out_shape]
    specs = [VM] * len(outs)
    return pl.pallas_call(
        kernel,
        out_shape=out_shape,
        in_specs=in_specs,
        out_specs=specs if isinstance(out_shape, (list, tuple)) else VM,
        compiler_params=pltpu.CompilerParams(vmem_limit_bytes=limit),
        cost_estimate=pl.CostEstimate(flops=flops, bytes_accessed=bytes_, transcendentals=0),
        **more,
    )(*args)


def in_hbm(a):
    return pltpu.with_memory_space_constraint(a, pltpu.HBM)


def in_vmem(a):
    return pltpu.with_memory_space_constraint(a, pltpu.VMEM)


def iota(shape, dim):
    return lax.broadcasted_iota(I32, shape, dim)


def placed(values, start):
    n = values.shape[1]
    spot = (iota((n, LANES), 1) == iota((n, LANES), 0) + start).astype(BF)
    return jnp.dot(values.astype(F32).astype(BF), spot, preferred_element_type=F32)


def pack(tokens, routes, gates, hint):
    rows, width = tokens.shape
    top = routes.shape[1]

    def kernel(t_in, r_in, g_in, x_out, t_v, r_v, g_v, sems):
        copies = [
            pltpu.make_async_copy(src, dst, sems.at[i])
            for i, (src, dst) in enumerate(((r_in, r_v), (g_in, g_v), (t_in, t_v)))
        ]
        for copy in copies:
            copy.start()
        for copy in copies:
            copy.wait()
        x_out[:, :width] = t_v[...]
        gate = g_v[...]
        meta = (
            placed(r_v[...], 0)
            + placed(lax.shift_right_logical(gate, 8), top)
            + placed(gate & 255, 2 * top)
        )
        x_out[:, width:] = meta.astype(BF)

    arrays = [in_hbm(a) for a in (tokens, routes, gates)]
    return run(
        kernel,
        sds((rows, width + LANES), BF),
        [HB] * len(arrays),
        arrays,
        flops=hint,
        scratch_shapes=[pltpu.VMEM(a.shape, a.dtype) for a in arrays]
        + [pltpu.SemaphoreType.DMA((len(arrays),))],
    )


def cat(pieces, after, hint=0):
    rows = pieces[0].shape[0]

    def kernel(*refs):
        for i in range(len(pieces)):
            refs[-1][i * rows : (i + 1) * rows] = refs[i][...]

    return run(
        kernel,
        sds((len(pieces) * rows,) + pieces[0].shape[1:], pieces[0].dtype),
        [VM] * (len(pieces) + len(after)),
        (*pieces, *after),
        flops=hint,
    )


def spread_scales(scales, after):
    def kernel(*refs):
        count = len(scales)
        ins, outs, held, sems = refs[:count], refs[count + 1 : 2 * count + 1], refs[2 * count + 1 : -1], refs[-1]
        copies = [
            pltpu.make_async_copy(src, dst, sems.at[i]) for i, (src, dst) in enumerate(zip(ins, held))
        ]
        for copy in copies:
            copy.start()
        for copy, src, dst in zip(copies, held, outs):
            copy.wait()
            for a in range(src.shape[0]):
                values = src[a].astype(F32)
                for b in range(src.shape[2]):
                    dst[a, b] = jnp.broadcast_to(values[:, b : b + 1], dst.shape[2:])

    return run(
        kernel,
        [sds((s.shape[0], s.shape[2], s.shape[1], LANES), F32) for s in scales],
        [HB] * len(scales) + [VM],
        (*[in_hbm(s) for s in scales], after),
        bytes_=1 << 20,
        scratch_shapes=[pltpu.VMEM(s.shape, s.dtype) for s in scales]
        + [pltpu.SemaphoreType.DMA((len(scales),))],
    )


def dispatch(x, width, top, rows_dev, experts, slots):
    rows = x.shape[0]
    per = slots // experts
    meta = x[:, width:].astype(F32)
    base = (lax.axis_index("seq") * experts).astype(F32)
    lane = iota((rows, LANES), 1)
    named = jnp.where(lane < experts, lane, -LANES).astype(F32) + base
    hits = jnp.zeros((rows, LANES), F32)
    gates = jnp.zeros((rows, LANES), F32)
    total = jnp.zeros((rows, 1), F32)
    for k in range(top):
        gate = meta[:, top + k : top + k + 1] * 256.0 + meta[:, 2 * top + k : 2 * top + k + 1]
        equal = meta[:, k : k + 1] == named
        hits = hits + jnp.where(equal, 1.0, 0.0)
        gates = gates + jnp.where(equal, gate, 0.0)
        total = total + gate
    weights = gates / total
    r0, r1 = iota((rows, rows), 0), iota((rows, rows), 1)
    earlier = ((r0 // rows_dev == r1 // rows_dev) & (r1 < r0)).astype(BF)
    rank = jnp.dot(earlier, hits.astype(BF), preferred_element_type=F32)
    grow = (iota((LANES, slots), 1) // per == iota((LANES, slots), 0)).astype(BF)
    wide_hits = jnp.dot(hits.astype(BF), grow, preferred_element_type=F32)
    wide_rank = jnp.dot(rank.astype(BF), grow, preferred_element_type=F32)
    spot = (iota((rows, slots), 1) % per - (iota((rows, slots), 0) // rows_dev) * CAP).astype(F32)
    sel = jnp.where((wide_hits > 0.5) & (wide_rank == spot), 1.0, 0.0).astype(BF)
    slot_rows = lax.dot_general(
        sel, x[:, :width], (((0,), (0,)), ((), ())), preferred_element_type=F32
    ).astype(BF)
    return sel, weights, slot_rows


def tile(parts):
    return jnp.concatenate([jnp.concatenate(row, axis=1) for row in parts], axis=0)


def scaled(block, scale, a, b, e):
    row = jnp.broadcast_to(scale[a, b, e : e + 1, :], (16, LANES)).astype(BF)
    return (block.reshape(QB // 16, 16, QB) * row[None]).reshape(QB, QB)


def half_products(xs_ref, gw, uw, gs, us, o_ref, half, chosen):
    experts, width, hidden = gw.shape
    n = hidden // 2 // QB
    per = xs_ref.shape[0] // experts
    columns = [(gw, gs, j) for j in range(n)] + [(uw, us, j) for j in range(n)]
    starts = [pl.multiple_of((half * n + j) * QB, QB) for j in range(n)]
    group, deep = 2, 2

    def block(w, scale, e, j, q):
        part = w[e, q * QB : (q + 1) * QB, pl.ds(starts[j], QB)]
        return scaled(part, scale, half * n + j, q, e)

    for row, e in enumerate(chosen):
        xs = xs_ref[e * per : (e + 1) * per, :]
        for at in range(0, len(columns), group):
            acc = jnp.zeros((per, group * QB), F32)
            for d in range(0, width // QB, deep):
                rhs = tile(
                    [
                        [block(w, s, e, j, q) for w, s, j in columns[at : at + group]]
                        for q in range(d, d + deep)
                    ]
                )
                acc = acc + jnp.dot(
                    xs[:, d * QB : (d + deep) * QB], rhs, preferred_element_type=F32
                )
            o_ref[row * per : (row + 1) * per, at * QB : (at + group) * QB] = acc.astype(o_ref.dtype)


def other_half(x, gw, uw, gs, us, top, rows_dev, block_count):
    experts, width, hidden = gw.shape
    slots = experts * block_count * CAP
    rows = block_count * rows_dev

    def kernel(x_ref, gw_ref, uw_ref, gs_ref, us_ref, o_ref, xs_ref, sel_ref, wt_ref):
        sel, weights, slot_rows = dispatch(x_ref[...], width, top, rows_dev, experts, slots)
        sel_ref[...] = sel
        wt_ref[...] = weights
        xs_ref[...] = slot_rows
        half = 1 - lax.rem(lax.axis_index("pool"), 2)
        half_products(xs_ref, gw_ref, uw_ref, gs_ref, us_ref, o_ref, half, range(experts))

    return run(
        kernel,
        [
            sds((slots, hidden), BF),
            sds((slots, width), BF),
            sds((rows, slots), BF),
            sds((rows, LANES), F32),
        ],
        [VM] * 5,
        (x, in_vmem(gw), in_vmem(uw), gs, us),
        limit=8 << 20,
        flops=NEAR,
        bytes_=NEAR,
    )


def own_half(xs, gw, uw, gs, us, chosen, after):
    experts, _, hidden = gw.shape
    slots = xs.shape[0] // experts * len(chosen)

    def kernel(xs_ref, gw_ref, uw_ref, gs_ref, us_ref, *rest):
        o_ref = rest[-1]
        half = lax.rem(lax.axis_index("pool"), 2)
        half_products(xs_ref, gw_ref, uw_ref, gs_ref, us_ref, o_ref, half, chosen)

    return run(
        kernel,
        sds((slots, hidden), F32),
        [VM] * (5 + len(after)),
        (xs, in_vmem(gw), in_vmem(uw), gs, us, *after),
        limit=8 << 20,
        flops=NEAR,
        bytes_=NEAR,
    )


def add_round(own, got, first, hint):
    rows = own.shape[0]

    def kernel(a_ref, b_ref, o_ref, r_ref):
        total = a_ref[...] + b_ref[first : first + rows].astype(F32)
        o_ref[...] = total
        r_ref[...] = total.astype(BF)

    return run(kernel, [sds(own.shape, F32), sds(own.shape, BF)], [VM] * 2, (own, got), flops=hint)


def activate(pairs):
    hidden = pairs[0][0].shape[1]
    rows = [own.shape[0] for own, _ in pairs]
    n = hidden // 2

    def kernel(*refs):
        first = 0
        for i, count in enumerate(rows):
            a_ref, b_ref = refs[2 * i : 2 * i + 2]
            gate = a_ref[:, :n] + b_ref[:, :n].astype(F32)
            up = a_ref[:, n:] + b_ref[:, n:].astype(F32)
            refs[-1][first : first + count] = (jax.nn.silu(gate) * up).astype(BF)
            first += count

    return run(
        kernel,
        sds((sum(rows), n), BF),
        [VM] * (2 * len(pairs)),
        [a for pair in pairs for a in pair],
    )


def spread_rows(h_ref, sel_ref, wt_ref, per, chosen):
    rows = sel_ref.shape[0]
    low = chosen[0] * per
    slots = h_ref.shape[0]
    sel = sel_ref[:, low : low + slots].astype(F32)
    owner = iota((rows, slots), 1) // per
    stack = jnp.concatenate(
        [jnp.where(owner == i, sel, 0.0) for i in range(len(chosen))], axis=0
    )
    spread = jnp.dot(stack.astype(BF), h_ref[...], preferred_element_type=F32)
    weights = wt_ref[...]
    return {
        e: (spread[i * rows : (i + 1) * rows] * weights[:, e : e + 1]).astype(BF)
        for i, e in enumerate(chosen)
    }


def down_kernel(hid, sel, wt, dw, ds, acc_in, chosen, other, parts_out):
    experts, hidden, width = dw.shape
    n = hidden // 2 // QB
    rows, slots = sel.shape
    per = slots // experts
    keep = rows // parts_out
    last = parts_out > 1
    given = [] if acc_in is None else [acc_in]
    group = 2
    pieces = [(e, j) for e in chosen for j in range(n)]
    deep = 2 if len(pieces) % 2 == 0 else 1

    def kernel(h_ref, sel_ref, wt_ref, dw_ref, ds_ref, *rest):
        given_refs, outs = rest[: len(given)], rest[len(given) :]
        half = lax.rem(lax.axis_index("pool"), 2)
        half = 1 - half if other else half
        parts = spread_rows(h_ref, sel_ref, wt_ref, per, chosen)
        starts = [pl.multiple_of((half * n + j) * QB, QB) for j in range(n)]

        def block(e, j, q):
            part = dw_ref[e, pl.ds(starts[j], QB), q * QB : (q + 1) * QB]
            return scaled(part, ds_ref, half * n + j, q, e)

        for c in range(0, width // QB, group):
            at = slice(c * QB, (c + group) * QB)
            acc = given_refs[0][:, at] if given else jnp.zeros((rows, group * QB), F32)
            for p in range(0, len(pieces), deep):
                some = pieces[p : p + deep]
                lhs = jnp.concatenate([parts[e][:, j * QB : (j + 1) * QB] for e, j in some], axis=1)
                rhs = tile([[block(e, j, q) for q in range(c, c + group)] for e, j in some])
                acc = acc + jnp.dot(lhs, rhs, preferred_element_type=F32)
            if last:
                outs[0][:, at] = acc[:keep]
                for g in range(1, parts_out):
                    outs[g][:, at] = acc[g * keep : (g + 1) * keep].astype(BF)
            else:
                outs[0][:, at] = acc

    return run(
        kernel,
        [sds((keep, width), F32)] + [sds((keep, width), BF)] * (parts_out - 1),
        [VM] * (5 + len(given)),
        (hid, sel, wt, in_vmem(dw), ds, *given),
        limit=8 << 20,
        flops=NEAR,
        bytes_=NEAR,
    )


def fold(own, got):
    rows, width = own.shape
    keep = rows // 2

    def kernel(a_ref, *rest):
        total = a_ref[...]
        for ref in rest[: len(got)]:
            total = total + ref[...].astype(F32)
        o_ref, s_ref = rest[len(got) :]
        o_ref[...] = total[:keep]
        s_ref[...] = total[keep:].astype(BF)

    return run(
        kernel,
        [sds((keep, width), F32), sds((keep, width), BF)],
        [VM] * (1 + len(got)),
        (own, *got),
    )


def finish(own, got):
    def kernel(a_ref, *rest):
        total = a_ref[...]
        for ref in rest[:-1]:
            total = total + ref[...].astype(F32)
        rest[-1][...] = total.astype(BF)

    return run(kernel, sds(own.shape, BF), [VM] * (1 + len(got)), (own, *got))


def swap(x, axis, bit):
    return lax.ppermute(x, axis, [(j, j ^ bit) for j in range(lax.axis_size(axis))])


def hop(x, *steps):
    n_seq, n_head = lax.axis_size("seq"), lax.axis_size("head")
    flip = {axis: sum(b for a, b in steps if a == axis) for axis in ("seq", "head")}
    pairs = [
        (s * n_head + h, (s ^ flip["seq"]) * n_head + (h ^ flip["head"]))
        for s in range(n_seq)
        for h in range(n_head)
    ]
    return lax.ppermute(x, ("seq", "head"), pairs)


def bits(count):
    return [1 << i for i in range(count.bit_length() - 1)]


def per_device(tokens, routes, gate_fixed, gw, uw, dw, gs, us, ds):
    n_seq, n_head, n_pool = (lax.axis_size(a) for a in ("seq", "head", "pool"))
    rows_dev, _ = tokens.shape
    top = routes.shape[1]
    hops = [("head", b) for b in reversed(bits(n_head))] + [("seq", b) for b in bits(n_seq)]

    x = pack(tokens, routes, gate_fixed, HINT * (gw.size + uw.size))
    scales = [gs.transpose(2, 0, 1), us.transpose(2, 0, 1), ds.transpose(1, 0, 2)]
    single, (a, b) = hops[:-2], hops[-2:]
    for step in single:
        got = hop(x, step)
        if scales:
            gs, us, ds = spread_scales(scales, x)
        x = cat([x, got], [gs] if scales else [], HINT * dw.size * LATE if scales else 0)
        scales = []
    far, near_a, near_b = hop(x, a, b), hop(x, a), hop(x, b)
    x = cat([x, near_a, near_b, far], [])

    send, xs, sel, wt = other_half(x, gw, uw, gs, us, top, rows_dev, n_seq * n_head)
    got = swap(send, "pool", 1)
    experts = gw.shape[0]
    per = xs.shape[0] // experts
    cut = experts * 6 // 8
    parts = [range(cut), range(cut, experts)] if cut else [range(experts)]
    steps = bits(n_pool)[1:]
    sums, after = [], []
    for i, part in enumerate(parts):
        own = own_half(xs, gw, uw, gs, us, part, after)
        first, hint = part[0] * per, HINT * dw.size
        arrived = got
        for bit in steps:
            own, send = add_round(own, arrived, first, hint if i + 1 == len(parts) else 0)
            arrived, first = swap(send, "pool", bit), 0
            after = [send]
        sums.append((own, arrived))
    everyone = range(experts)
    hid = activate(sums)
    other = swap(hid, "pool", 1)
    (acc,) = down_kernel(hid, sel, wt, dw, ds, None, everyone, False, 1)
    acc, to_a, to_b, to_far = down_kernel(other, sel, wt, dw, ds, acc, everyone, True, 4)
    far, near_a, near_b = hop(to_far, a, b), hop(to_a, a), hop(to_b, b)
    got = [far, near_b, near_a]
    for step in reversed(single):
        acc, send = fold(acc, got)
        got = [hop(send, step)]
    return finish(acc, got)


def solution(mesh):
    return jax.shard_map(
        per_device,
        mesh=mesh,
        in_specs=(
            P(("seq", "head"), "pool"),
            P(("seq", "head"), None),
            P(("seq", "head"), None),
            P("seq", "pool", "head"),
            P("seq", "pool", "head"),
            P("seq", "head", "pool"),
            P("seq", "pool", "head"),
            P("seq", "pool", "head"),
            P("seq", "head", "pool"),
        ),
        out_specs=P(("seq", "head"), "pool"),
        check_vma=False,
    )
```

```python
import jax
import jax.numpy as jnp
from jax import lax
from jax.experimental import pallas as pl
from jax.experimental.pallas import tpu as pltpu
from jax.sharding import PartitionSpec as P

QB = 128
CAP = 2
HINT = 1000
NEAR = 1 << 16
LATE = 0
LANES = 128
BF = jnp.bfloat16
F32 = jnp.float32
I32 = jnp.int32

VM = pl.BlockSpec(memory_space=pltpu.VMEM)
HB = pl.BlockSpec(memory_space=pltpu.HBM)


def sds(shape, dtype):
    return jax.ShapeDtypeStruct(shape, dtype)


def run(kernel, out_shape, in_specs, args, limit=2 << 20, flops=0, bytes_=0, **more):
    outs = out_shape if isinstance(out_shape, (list, tuple)) else [out_shape]
    specs = [VM] * len(outs)
    return pl.pallas_call(
        kernel,
        out_shape=out_shape,
        in_specs=in_specs,
        out_specs=specs if isinstance(out_shape, (list, tuple)) else VM,
        compiler_params=pltpu.CompilerParams(vmem_limit_bytes=limit),
        cost_estimate=pl.CostEstimate(flops=flops, bytes_accessed=bytes_, transcendentals=0),
        **more,
    )(*args)


def in_hbm(a):
    return pltpu.with_memory_space_constraint(a, pltpu.HBM)


def in_vmem(a):
    return pltpu.with_memory_space_constraint(a, pltpu.VMEM)


def iota(shape, dim):
    return lax.broadcasted_iota(I32, shape, dim)


def placed(values, start):
    n = values.shape[1]
    spot = (iota((n, LANES), 1) == iota((n, LANES), 0) + start).astype(BF)
    return jnp.dot(values.astype(F32).astype(BF), spot, preferred_element_type=F32)


def pack(tokens, routes, gates, hint):
    rows, width = tokens.shape
    top = routes.shape[1]

    def kernel(t_in, r_in, g_in, x_out, r_v, g_v, sems):
        copies = [
            pltpu.make_async_copy(src, dst, sems.at[i])
            for i, (src, dst) in enumerate(((r_in, r_v), (g_in, g_v), (t_in, x_out.at[:, pl.ds(0, width)])))
        ]
        for copy in copies:
            copy.start()
        for copy in copies[:2]:
            copy.wait()
        gate = g_v[...]
        meta = (
            placed(r_v[...], 0)
            + placed(lax.shift_right_logical(gate, 8), top)
            + placed(gate & 255, 2 * top)
        )
        x_out[:, width:] = meta.astype(BF)
        copies[2].wait()

    arrays = [in_hbm(a) for a in (tokens, routes, gates)]
    return run(
        kernel,
        sds((rows, width + LANES), BF),
        [HB] * len(arrays),
        arrays,
        flops=hint,
        scratch_shapes=[pltpu.VMEM(a.shape, a.dtype) for a in arrays[1:]]
        + [pltpu.SemaphoreType.DMA((len(arrays),))],
    )


def cat(pieces, after, hint=0):
    rows = pieces[0].shape[0]

    def kernel(*refs):
        for i in range(len(pieces)):
            refs[-1][i * rows : (i + 1) * rows] = refs[i][...]

    return run(
        kernel,
        sds((len(pieces) * rows,) + pieces[0].shape[1:], pieces[0].dtype),
        [VM] * (len(pieces) + len(after)),
        (*pieces, *after),
        flops=hint,
    )


def spread_scales(scales, after, hint):
    def kernel(*refs):
        count = len(scales)
        ins, outs, held, sems = refs[:count], refs[count + 1 : 2 * count + 1], refs[2 * count + 1 : -1], refs[-1]
        copies = [
            pltpu.make_async_copy(src, dst, sems.at[i]) for i, (src, dst) in enumerate(zip(ins, held))
        ]
        for copy in copies:
            copy.start()
        for copy, src, dst in zip(copies, held, outs):
            copy.wait()
            for a in range(src.shape[0]):
                values = src[a].astype(F32)
                for b in range(src.shape[2]):
                    dst[a, b] = jnp.broadcast_to(values[:, b : b + 1], dst.shape[2:])

    return run(
        kernel,
        [sds((s.shape[0], s.shape[2], s.shape[1], LANES), F32) for s in scales],
        [HB] * len(scales) + [VM],
        (*[in_hbm(s) for s in scales], after),
        flops=hint,
        bytes_=1 << 20,
        scratch_shapes=[pltpu.VMEM(s.shape, s.dtype) for s in scales]
        + [pltpu.SemaphoreType.DMA((len(scales),))],
    )


def dispatch(x, width, top, rows_dev, experts, slots):
    rows = x.shape[0]
    per = slots // experts
    meta = x[:, width:].astype(F32)
    base = (lax.axis_index("seq") * experts).astype(F32)
    lane = iota((rows, LANES), 1)
    named = jnp.where(lane < experts, lane, -LANES).astype(F32) + base
    hits = jnp.zeros((rows, LANES), F32)
    gates = jnp.zeros((rows, LANES), F32)
    total = jnp.zeros((rows, 1), F32)
    for k in range(top):
        gate = meta[:, top + k : top + k + 1] * 256.0 + meta[:, 2 * top + k : 2 * top + k + 1]
        equal = meta[:, k : k + 1] == named
        hits = hits + jnp.where(equal, 1.0, 0.0)
        gates = gates + jnp.where(equal, gate, 0.0)
        total = total + gate
    weights = gates / total
    r0, r1 = iota((rows, rows), 0), iota((rows, rows), 1)
    earlier = ((r0 // rows_dev == r1 // rows_dev) & (r1 < r0)).astype(BF)
    rank = jnp.dot(earlier, hits.astype(BF), preferred_element_type=F32)
    grow = (iota((LANES, slots), 1) // per == iota((LANES, slots), 0)).astype(BF)
    wide_hits = jnp.dot(hits.astype(BF), grow, preferred_element_type=F32)
    wide_rank = jnp.dot(rank.astype(BF), grow, preferred_element_type=F32)
    spot = (iota((rows, slots), 1) % per - (iota((rows, slots), 0) // rows_dev) * CAP).astype(F32)
    sel = jnp.where((wide_hits > 0.5) & (wide_rank == spot), 1.0, 0.0).astype(BF)
    slot_rows = lax.dot_general(
        sel, x[:, :width], (((0,), (0,)), ((), ())), preferred_element_type=F32
    ).astype(BF)
    return sel, weights, slot_rows


def tile(parts):
    return jnp.concatenate([jnp.concatenate(row, axis=1) for row in parts], axis=0)


def scaled(block, scale, a, b, e):
    row = jnp.broadcast_to(scale[a, b, e : e + 1, :], (16, LANES)).astype(BF)
    return (block.reshape(QB // 16, 16, QB) * row[None]).reshape(QB, QB)


def half_products(xs_ref, gw, uw, gs, us, o_ref, half, chosen):
    experts, width, hidden = gw.shape
    n = hidden // 2 // QB
    per = xs_ref.shape[0] // experts
    columns = [(gw, gs, j) for j in range(n)] + [(uw, us, j) for j in range(n)]
    starts = [pl.multiple_of((half * n + j) * QB, QB) for j in range(n)]
    group, deep = 2, 2

    def block(w, scale, e, j, q):
        part = w[e, q * QB : (q + 1) * QB, pl.ds(starts[j], QB)]
        return scaled(part, scale, half * n + j, q, e)

    for row, e in enumerate(chosen):
        xs = xs_ref[e * per : (e + 1) * per, :]
        for at in range(0, len(columns), group):
            acc = jnp.zeros((per, group * QB), F32)
            for d in range(0, width // QB, deep):
                rhs = tile(
                    [
                        [block(w, s, e, j, q) for w, s, j in columns[at : at + group]]
                        for q in range(d, d + deep)
                    ]
                )
                acc = acc + jnp.dot(
                    xs[:, d * QB : (d + deep) * QB], rhs, preferred_element_type=F32
                )
            o_ref[row * per : (row + 1) * per, at * QB : (at + group) * QB] = acc.astype(o_ref.dtype)


def other_half(x, gw, uw, gs, us, top, rows_dev, block_count):
    experts, width, hidden = gw.shape
    slots = experts * block_count * CAP
    rows = block_count * rows_dev

    def kernel(x_ref, gw_ref, uw_ref, gs_ref, us_ref, o_ref, xs_ref, sel_ref, wt_ref):
        sel, weights, slot_rows = dispatch(x_ref[...], width, top, rows_dev, experts, slots)
        sel_ref[...] = sel
        wt_ref[...] = weights
        xs_ref[...] = slot_rows
        half = 1 - lax.rem(lax.axis_index("pool"), 2)
        half_products(xs_ref, gw_ref, uw_ref, gs_ref, us_ref, o_ref, half, range(experts))

    return run(
        kernel,
        [
            sds((slots, hidden), BF),
            sds((slots, width), BF),
            sds((rows, slots), BF),
            sds((rows, LANES), F32),
        ],
        [VM] * 5,
        (x, in_vmem(gw), in_vmem(uw), gs, us),
        limit=8 << 20,
        flops=NEAR,
        bytes_=NEAR,
    )


def own_half(xs, gw, uw, gs, us, chosen, after):
    experts, _, hidden = gw.shape
    slots = xs.shape[0] // experts * len(chosen)

    def kernel(xs_ref, gw_ref, uw_ref, gs_ref, us_ref, *rest):
        o_ref = rest[-1]
        half = lax.rem(lax.axis_index("pool"), 2)
        half_products(xs_ref, gw_ref, uw_ref, gs_ref, us_ref, o_ref, half, chosen)

    return run(
        kernel,
        sds((slots, hidden), F32),
        [VM] * (5 + len(after)),
        (xs, in_vmem(gw), in_vmem(uw), gs, us, *after),
        limit=8 << 20,
        flops=NEAR,
        bytes_=NEAR,
    )


def add_round(own, got, first, hint):
    rows = own.shape[0]

    def kernel(a_ref, b_ref, o_ref, r_ref):
        total = a_ref[...] + b_ref[first : first + rows].astype(F32)
        o_ref[...] = total
        r_ref[...] = total.astype(BF)

    return run(kernel, [sds(own.shape, F32), sds(own.shape, BF)], [VM] * 2, (own, got), flops=hint)


def activate(pairs):
    hidden = pairs[0][0].shape[1]
    rows = [own.shape[0] for own, _ in pairs]
    n = hidden // 2

    def kernel(*refs):
        first = 0
        for i, count in enumerate(rows):
            a_ref, b_ref = refs[2 * i : 2 * i + 2]
            gate = a_ref[:, :n] + b_ref[:, :n].astype(F32)
            up = a_ref[:, n:] + b_ref[:, n:].astype(F32)
            refs[-1][first : first + count] = (jax.nn.silu(gate) * up).astype(BF)
            first += count

    return run(
        kernel,
        sds((sum(rows), n), BF),
        [VM] * (2 * len(pairs)),
        [a for pair in pairs for a in pair],
    )


def spread_rows(h_ref, sel_ref, wt_ref, per, chosen):
    rows = sel_ref.shape[0]
    low = chosen[0] * per
    slots = h_ref.shape[0]
    sel = sel_ref[:, low : low + slots].astype(F32)
    owner = iota((rows, slots), 1) // per
    stack = jnp.concatenate(
        [jnp.where(owner == i, sel, 0.0) for i in range(len(chosen))], axis=0
    )
    spread = jnp.dot(stack.astype(BF), h_ref[...], preferred_element_type=F32)
    weights = wt_ref[...]
    return {
        e: (spread[i * rows : (i + 1) * rows] * weights[:, e : e + 1]).astype(BF)
        for i, e in enumerate(chosen)
    }


def down_kernel(hid, sel, wt, dw, ds, acc_in, chosen, other, parts_out):
    experts, hidden, width = dw.shape
    n = hidden // 2 // QB
    rows, slots = sel.shape
    per = slots // experts
    keep = rows // parts_out
    last = parts_out > 1
    given = [] if acc_in is None else [acc_in]
    group = 2
    pieces = [(e, j) for e in chosen for j in range(n)]
    deep = 2 if len(pieces) % 2 == 0 else 1

    def kernel(h_ref, sel_ref, wt_ref, dw_ref, ds_ref, *rest):
        given_refs, outs = rest[: len(given)], rest[len(given) :]
        half = lax.rem(lax.axis_index("pool"), 2)
        half = 1 - half if other else half
        parts = spread_rows(h_ref, sel_ref, wt_ref, per, chosen)
        starts = [pl.multiple_of((half * n + j) * QB, QB) for j in range(n)]

        def block(e, j, q):
            part = dw_ref[e, pl.ds(starts[j], QB), q * QB : (q + 1) * QB]
            return scaled(part, ds_ref, half * n + j, q, e)

        for c in range(0, width // QB, group):
            at = slice(c * QB, (c + group) * QB)
            acc = given_refs[0][:, at] if given else jnp.zeros((rows, group * QB), F32)
            for p in range(0, len(pieces), deep):
                some = pieces[p : p + deep]
                lhs = jnp.concatenate([parts[e][:, j * QB : (j + 1) * QB] for e, j in some], axis=1)
                rhs = tile([[block(e, j, q) for q in range(c, c + group)] for e, j in some])
                acc = acc + jnp.dot(lhs, rhs, preferred_element_type=F32)
            if last:
                outs[0][:, at] = acc[:keep]
                for g in range(1, parts_out):
                    outs[g][:, at] = acc[g * keep : (g + 1) * keep].astype(BF)
            else:
                outs[0][:, at] = acc

    return run(
        kernel,
        [sds((keep, width), F32)] + [sds((keep, width), BF)] * (parts_out - 1),
        [VM] * (5 + len(given)),
        (hid, sel, wt, in_vmem(dw), ds, *given),
        limit=8 << 20,
        flops=NEAR,
        bytes_=NEAR,
    )


def fold(own, got):
    rows, width = own.shape
    keep = rows // 2

    def kernel(a_ref, *rest):
        total = a_ref[...]
        for ref in rest[: len(got)]:
            total = total + ref[...].astype(F32)
        o_ref, s_ref = rest[len(got) :]
        o_ref[...] = total[:keep]
        s_ref[...] = total[keep:].astype(BF)

    return run(
        kernel,
        [sds((keep, width), F32), sds((keep, width), BF)],
        [VM] * (1 + len(got)),
        (own, *got),
    )


def finish(own, got):
    def kernel(a_ref, *rest):
        total = a_ref[...]
        for ref in rest[:-1]:
            total = total + ref[...].astype(F32)
        rest[-1][...] = total.astype(BF)

    return run(kernel, sds(own.shape, BF), [VM] * (1 + len(got)), (own, *got))


def swap(x, axis, bit):
    return lax.ppermute(x, axis, [(j, j ^ bit) for j in range(lax.axis_size(axis))])


def hop(x, *steps):
    n_seq, n_head = lax.axis_size("seq"), lax.axis_size("head")
    flip = {axis: sum(b for a, b in steps if a == axis) for axis in ("seq", "head")}
    pairs = [
        (s * n_head + h, (s ^ flip["seq"]) * n_head + (h ^ flip["head"]))
        for s in range(n_seq)
        for h in range(n_head)
    ]
    return lax.ppermute(x, ("seq", "head"), pairs)


def bits(count):
    return [1 << i for i in range(count.bit_length() - 1)]


def per_device(tokens, routes, gate_fixed, gw, uw, dw, gs, us, ds):
    n_seq, n_head, n_pool = (lax.axis_size(a) for a in ("seq", "head", "pool"))
    rows_dev, _ = tokens.shape
    top = routes.shape[1]
    hops = [("head", b) for b in reversed(bits(n_head))] + [("seq", b) for b in bits(n_seq)]

    x = pack(tokens, routes, gate_fixed, NEAR)
    scales = [gs.transpose(2, 0, 1), us.transpose(2, 0, 1), ds.transpose(1, 0, 2)]
    single, (a, b) = hops[:-2], hops[-2:]
    for step in single:
        got = hop(x, step)
        if scales:
            gs, us, ds = spread_scales(scales, x, HINT * (gw.size + uw.size))
        x = cat([x, got], [gs] if scales else [], HINT * dw.size * LATE if scales else 0)
        scales = []
    far, near_a, near_b = hop(x, a, b), hop(x, a), hop(x, b)
    x = cat([x, near_a, near_b, far], [])

    send, xs, sel, wt = other_half(x, gw, uw, gs, us, top, rows_dev, n_seq * n_head)
    got = swap(send, "pool", 1)
    experts = gw.shape[0]
    per = xs.shape[0] // experts
    cut = experts * 5 // 8
    parts = [range(cut), range(cut, experts)] if cut else [range(experts)]
    steps = bits(n_pool)[1:]
    sums, after = [], []
    for i, part in enumerate(parts):
        own = own_half(xs, gw, uw, gs, us, part, after)
        first, hint = part[0] * per, HINT * dw.size
        arrived = got
        for bit in steps:
            own, send = add_round(own, arrived, first, hint if i + 1 == len(parts) else 0)
            arrived, first = swap(send, "pool", bit), 0
            after = [send]
        sums.append((own, arrived))
    everyone = range(experts)
    hid = activate(sums)
    other = swap(hid, "pool", 1)
    (acc,) = down_kernel(hid, sel, wt, dw, ds, None, everyone, False, 1)
    acc, to_a, to_b, to_far = down_kernel(other, sel, wt, dw, ds, acc, everyone, True, 4)
    far, near_a, near_b = hop(to_far, a, b), hop(to_a, a), hop(to_b, b)
    got = [far, near_b, near_a]
    for step in reversed(single):
        acc, send = fold(acc, got)
        got = [hop(send, step)]
    return finish(acc, got)


def solution(mesh):
    return jax.shard_map(
        per_device,
        mesh=mesh,
        in_specs=(
            P(("seq", "head"), "pool"),
            P(("seq", "head"), None),
            P(("seq", "head"), None),
            P("seq", "pool", "head"),
            P("seq", "pool", "head"),
            P("seq", "head", "pool"),
            P("seq", "pool", "head"),
            P("seq", "pool", "head"),
            P("seq", "head", "pool"),
        ),
        out_specs=P(("seq", "head"), "pool"),
        check_vma=False,
    )
```
